256 devices in a mesh: row: 16 (over y, x), col: 16 (over z, core).
Axes of the slice: x: 4, y: 4, z: 8, core: 2. Of those that a mesh axis runs over, the one named last changes fastest.
Arguments:
- trail_grad: float32 [16384, 16384], P('row', 'col'), may hold values from -20 to 20, as said below
- factor_rows: float32 [16384, 768], P('col', 'row'), may hold values from -0.046875 to 0.046875
- factor_top: float32 [768, 768], replicated, may hold values from -1 to 2, as said below
- rows_grad: float32 [16384, 768], P(('row', 'col')), may hold values from -6 to 6
- top_grad: float32 [768, 768], replicated, may hold values from -6 to 6, as said below
Outputs:
- rows_adjoint: float32 [16384, 768], P(('row', 'col'))
- top_adjoint: float32 [768, 768], replicated
The draws below stay inside these ranges and needn't reach their ends.
Inputs may be any that keep to these rules, and one draw needn't show every extreme that they name: trail_grad is symmetric once both of its orders are reverted. factor_top is lower triangular with its diagonal between 1 and 2. top_grad is lower triangular.
All inputs are finite; a program needn't handle non-finite values.
Results may differ from the reference program's by a relative error of at most 0.0001.
Values sent between devices are 32-bit elements; how exact they have to be, the bound alone decides.
A program may use at most 64 MiB of HBM per device.

```python
import jax
import jax.numpy as jnp
from jax import lax

M = 16384
NB = 256
NP = 3
CB = 128
PW = 768
N_ROW = 16
N_COL = 16


def stored_order_drawn(matrix, owners):
    tile_count = matrix.shape[0] // (owners * CB)
    return matrix.reshape(tile_count, owners, CB, matrix.shape[1]).transpose(1, 0, 2, 3).reshape(matrix.shape)


def draw_trail_grad(key, part):
    first = jax.random.fold_in(jax.random.fold_in(key, 11), 0)
    base = jnp.clip(jax.random.normal(first, (M, M), jnp.float32), -6.0, 6.0)
    symmetric = (base + base.T) * 0.35355339
    rows_done = stored_order_drawn(symmetric, N_ROW)
    return stored_order_drawn(rows_done.T, N_COL).T


def draw_factor_top(key, part):
    first, second = jax.random.split(jax.random.fold_in(key, 23))
    panel_width = NP * NB
    row_ids = lax.broadcasted_iota(jnp.int32, (panel_width, panel_width), 0)
    col_ids = lax.broadcasted_iota(jnp.int32, (panel_width, panel_width), 1)
    noise = jnp.clip(jax.random.normal(first, (panel_width, panel_width), jnp.float32), -4.0, 4.0)
    diag_values = jax.random.uniform(second, (panel_width, panel_width), jnp.float32, 1.0, 2.0)
    same_panel = row_ids // NB == col_ids // NB
    lower_part = jnp.where(same_panel, 0.45 * noise, noise) / jnp.sqrt(jnp.float32(NB))
    lower_part = jnp.clip(lower_part, -1.0, 1.0)
    return jnp.where(row_ids == col_ids, diag_values, jnp.where(row_ids > col_ids, lower_part, 0.0))


def draw_top_grad(key, part):
    first = jax.random.fold_in(key, 37)
    panel_width = NP * NB
    values = jnp.clip(jax.random.normal(first, (panel_width, panel_width), jnp.float32), -6.0, 6.0)
    return jnp.tril(values)


def shard_levels(own_key, extent, cuts, least, high):
    def one(axis_at, shards_of):
        heights = jax.random.uniform(jax.random.fold_in(jax.random.fold_in(own_key, 6), axis_at), (shards_of,), jnp.float32, least / len(cuts), high / len(cuts))
        return jnp.repeat(jnp.exp(heights), extent[axis_at] // shards_of).reshape((-1,) + (1,) * (len(extent) - axis_at - 1))

    level = one(*cuts[0])
    for cut in cuts[1:]:
        level = level * one(*cut)
    return level


def bell_draw(key, shape, scale, reach, pieces=(), kind=jnp.bfloat16):
    result = jax.random.normal(key, shape, jnp.float32) * scale
    if len(pieces) > 0:
        result = shard_levels(key, shape, pieces, -0.22, 0.18) * result
    return jnp.clip(result, min=-reach, max=reach).astype(kind)


def setup_inputs(seed: int = 0) -> dict:
    splits = jax.random.split(jax.random.key(seed), 6)
    return {
        "trail_grad": draw_trail_grad(jax.random.fold_in(splits[5], 71), 0),
        "factor_rows": bell_draw(splits[1], (M, PW), M ** -0.5, 0.046875, ((0, 16), (1, 16)), jnp.float32),
        "factor_top": draw_factor_top(jax.random.fold_in(splits[5], 71), 0),
        "rows_grad": bell_draw(splits[3], (M, PW), 1.0, 6.0, ((0, 256),), jnp.float32),
        "top_grad": draw_top_grad(jax.random.fold_in(splits[5], 71), 0),
    }


exact_dots = lax.Precision.HIGHEST

def natural_order(stored, owners):
    tile_count = stored.shape[0] // (owners * CB)
    return stored.reshape(owners, tile_count, CB, stored.shape[1]).transpose(1, 0, 2, 3).reshape(stored.shape)

def stored_order(matrix, owners):
    tile_count = matrix.shape[0] // (owners * CB)
    return matrix.reshape(tile_count, owners, CB, matrix.shape[1]).transpose(1, 0, 2, 3).reshape(matrix.shape)

def product(left, right):
    return jnp.dot(left.astype(jnp.float32), right.astype(jnp.float32), precision=exact_dots, preferred_element_type=jnp.float32)

def halve_diagonal(matrix):
    order = matrix.shape[0]
    row_ids = lax.broadcasted_iota(jnp.int32, (order, order), 0)
    col_ids = lax.broadcasted_iota(jnp.int32, (order, order), 1)
    return jnp.where(row_ids > col_ids, matrix, jnp.where(row_ids == col_ids, 0.5 * matrix, 0.0))

def cholesky_adjoint(factor, inverse, gradient):
    inner = halve_diagonal(product(factor.T, gradient))
    middle = product(product(inverse.T, inner), inverse)
    return halve_diagonal(middle + middle.T)

def reference(trail_grad, factor_rows, factor_top, rows_grad, top_grad):
    panel_width = NP * NB
    twice = 2.0 * product(trail_grad, factor_rows)
    trail_part = natural_order(twice, N_ROW)
    factor_nat = natural_order(factor_rows, N_COL)
    grad_nat = natural_order(rows_grad, N_ROW)
    row_index = lax.broadcasted_iota(jnp.int32, (panel_width, NB), 0)
    identity = jnp.eye(NB, dtype=jnp.float32)
    adj_rows = jnp.zeros((M, panel_width), jnp.float32)
    adj_top = jnp.zeros((panel_width, panel_width), jnp.float32)
    for which_panel in reversed(range(NP)):
        col_start = which_panel * NB
        col_end = col_start + NB
        below_diag = jnp.where(row_index >= col_end, factor_top[:, col_start:col_end], 0.0)
        diag_block = factor_top[col_start:col_end, col_start:col_end]
        inverse = jax.scipy.linalg.solve_triangular(diag_block, identity, lower=True)
        rows_cbar = grad_nat[:, col_start:col_end] - trail_part[:, col_start:col_end] - product(adj_rows, below_diag)
        cross_part = product(adj_rows.T, factor_nat[:, col_start:col_end])
        top_masked = jnp.where(row_index >= col_end, top_grad[:, col_start:col_end], 0.0)
        top_cbar = top_masked - (product(adj_top + adj_top.T, below_diag) + cross_part)
        rows_adj = product(rows_cbar, inverse)
        top_adj = product(top_cbar, inverse)
        diag_grad = jnp.tril(top_grad[col_start:col_end, col_start:col_end] - product(top_adj.T, below_diag) - product(rows_adj.T, factor_nat[:, col_start:col_end]))
        diag_adjoint = cholesky_adjoint(diag_block, inverse, diag_grad)
        adj_rows = adj_rows.at[:, col_start:col_end].set(rows_adj)
        adj_top = adj_top.at[:, col_start:col_end].set(top_adj.at[col_start:col_end].set(diag_adjoint))
    return (stored_order(adj_rows, N_ROW), adj_top)
```

```python
import jax
import jax.numpy as jnp
from jax import lax
from jax.experimental import pallas as pl
from jax.experimental.pallas import tpu as pltpu
from jax.sharding import PartitionSpec as P

MESH = pl.DeviceIdType.MESH
F32, BF16 = jnp.float32, jnp.bfloat16
HIGHEST = lax.Precision.HIGHEST
NX, NY, NZ = 4, 4, 8
BLOCK, HALF, WIDTH = 256, 128, 768
CHUNK, PIECE = 48, 24
GROUP, SUB = 192, 96
OFFSETS = (0, 768, 1280)
SEMAPHORES = 200


def contract(left, right, dims, precision=None):
    return lax.dot_general(left, right, (dims, ((), ())), precision=precision, preferred_element_type=F32)


def split(value):
    high = value.astype(BF16)
    return high, (value - high.astype(F32)).astype(BF16)


def dot3(left, right, dims=((1,), (0,))):
    left_high, left_low = split(left)
    right_high, right_low = split(right)
    return (
        contract(left_low, right_high, dims)
        + contract(left_high, right_low, dims)
        + contract(left_high, right_high, dims)
    )


def dot6(left, right):
    return contract(left, right, ((1,), (0,)), HIGHEST)


def iota(shape, dim):
    return lax.broadcasted_iota(jnp.int32, shape, dim)


def aligned(index, unit):
    return pl.multiple_of(index * unit, unit)


def kernel(trail, factor, lower, grad, top, out_rows, out_top, strail, s_high, s_low, f_all, zt, cx, zc, r_left, r_right, low, topv,
           inv, inv_t, cmat, mmat, xmat, gbuf, p_hat, p_rows, f_own, wst, r_a1, r_a2, a1, a2, r_b1, r_b2, b1, b2, r_c1, r_c2, c1, c2,
           wfull, local_sem, send_sem, recv_sem):
    row, col = lax.axis_index("row"), lax.axis_index("col")
    y, x = lax.div(row, NX), lax.rem(row, NX)
    z, k = lax.div(col, 2), lax.rem(col, 2)
    other = 1 - k

    def at_x(d):
        return (y * NX + lax.rem(x + d + NX, NX), col)

    def at_y(d):
        return (lax.rem(y + d + NY, NY) * NX + x, col)

    def at_z(d):
        return (row, lax.rem(z + d + NZ, NZ) * 2 + k)

    partner = (row, z * 2 + other)
    count = [0]
    pending = []

    def push(src, dst, device):
        slot = count[0]
        count[0] += 1
        copy = pltpu.make_async_remote_copy(
            src_ref=src, dst_ref=dst, send_sem=send_sem.at[slot], recv_sem=recv_sem.at[slot], device_id=device, device_id_type=MESH
        )
        copy.start()
        pending.append(copy)
        return copy

    local = [
        pltpu.make_async_copy(factor, f_all.at[pl.ds(aligned(row, CHUNK), CHUNK)], local_sem.at[0]),
        pltpu.make_async_copy(grad, gbuf.at[pl.ds(aligned(k, 64), 64)], local_sem.at[1]),
        pltpu.make_async_copy(trail, strail, local_sem.at[2]),
        pltpu.make_async_copy(lower, low, local_sem.at[3]),
        pltpu.make_async_copy(top, topv, local_sem.at[4]),
    ]
    for copy in local:
        copy.start()

    barrier = pltpu.get_barrier_semaphore()

    def greet(device):
        pl.semaphore_signal(barrier, inc=1, device_id=device, device_id_type=MESH)

    for d in range(1, NX):
        greet(at_x(d))
    for d in range(1, NY):
        greet(at_y(d))
    for d in range(1, NZ):
        greet(at_z(d))
    greet(partner)

    @pl.when(row != col)
    def _():
        greet((col, row))
        pl.semaphore_wait(barrier, 15)

    @pl.when(row == col)
    def _():
        pl.semaphore_wait(barrier, 14)

    local[0].wait()
    local[1].wait()

    rings = {"x": at_x, "y": at_y}

    def piece(ring, item, shift):
        if ring == "x":
            owner_x, owner_y = lax.rem(x + shift + NX, NX), y if item == 0 else lax.rem(y + item - 1, NY)
            offset = 0 if item == 0 else PIECE
        else:
            owner_y, owner_x = lax.rem(y + shift + NY, NY), x if item == 0 else lax.rem(x + item - 1, NX)
            offset = PIECE if item == 0 else 0
        return pl.ds(pl.multiple_of((owner_y * NX + owner_x) * CHUNK + offset, 8), PIECE)

    full, halves = {}, {}

    def send(ring, item):
        rows = f_all.at[piece(ring, item, 0)]
        full[ring, item] = [push(rows, rows, rings[ring](1)), push(rows, rows, rings[ring](-1))]

    def forward(ring, item):
        from_left, from_right = full[ring, item]
        from_left.wait_recv()
        rows = f_all.at[piece(ring, item, -1), pl.ds(0, 512)]
        right = push(rows, rows, rings[ring](1))
        from_right.wait_recv()
        rows = f_all.at[piece(ring, item, 1), pl.ds(512, 512)]
        halves[ring, item] = [right, push(rows, rows, rings[ring](-1))]

    def settle(ring, item):
        for copy in halves[ring, item]:
            copy.wait_recv()

    send("x", 0), send("y", 0), send("x", 1), send("y", 1)
    grad_copy = push(gbuf.at[pl.ds(aligned(k, 64), 64)], gbuf.at[pl.ds(aligned(k, 64), 64)], partner)

    local[3].wait()
    inverse_diagonals(low, inv)
    forward("x", 0), forward("y", 0)
    send("x", 2), send("y", 2), send("x", 4), send("y", 4)
    local[2].wait()

    @pl.loop(0, 8)
    def _(step):
        rows = pl.ds(aligned(step, 128), 128)
        s_high[rows], s_low[rows] = split(strail[rows])

    forward("x", 1), forward("y", 1)
    settle("x", 0), settle("y", 0)
    send("x", 3), send("y", 3)
    inverse_blocks(low, inv)
    forward("x", 2), forward("y", 2), forward("x", 4), forward("y", 4)
    settle("x", 1)

    def multiply(j):
        rows = pl.ds(aligned(lax.rem(y + j, NY), GROUP), GROUP)
        f_high, f_low = split(f_all[rows])

        @pl.loop(0, 4)
        def _(step):
            part = pl.ds(aligned(step, BLOCK), BLOCK)
            dims = ((1,), (1,))
            zt[j, :, part] = (
                contract(f_low, s_high[part], dims) + contract(f_high, s_low[part], dims) + contract(f_high, s_high[part], dims)
            )

    crossing = {}

    def cross(j):
        crossing[j] = push(zt.at[j, pl.ds(aligned(other, SUB), SUB)], cx.at[j], partner)

    lefts, rights = {}, {}

    def begin(j):
        crossing[j].wait_recv()
        own = pl.ds(aligned(k, SUB), SUB)
        for d in range(NZ):
            lanes = pl.ds(128 * d, 128)
            zc[j, d] = zt[j, own, lanes] + cx[j, :, lanes]
        far = lax.rem(z + 4, NZ)
        lefts[j] = push(zc.at[j, far, pl.ds(0, 48)], r_left.at[j, 0, pl.ds(0, 48)], at_z(-1))
        rights[j] = push(zc.at[j, far, pl.ds(48, 48)], r_right.at[j, 0, pl.ds(48, 48)], at_z(1))

    def travel(j, step):
        to_left, to_right = lax.rem(z + 3 + step, NZ), lax.rem(z + 5 - step, NZ)
        lefts[j].wait_recv()
        if step == 2:
            zc[j, to_left, 0:48] += r_left[j, 0, 0:48]
        else:
            zc[j, to_left] += r_left[j, step - 2]
        lefts[j] = push(zc.at[j, to_left], r_left.at[j, step - 1], at_z(-1))
        rights[j].wait_recv()
        if step == 2:
            zc[j, to_right, 48:96] += r_right[j, 0, 48:96]
        else:
            zc[j, to_right] += r_right[j, step - 2]
        rights[j] = push(zc.at[j, to_right], r_right.at[j, step - 1], at_z(1))

    shares = []

    def arrive(j):
        lefts[j].wait_recv()
        rights[j].wait_recv()
        rows = pl.ds(pl.multiple_of(lax.rem(y + j, NY) * GROUP + k * SUB, 8), SUB)
        p_hat[rows] = p_hat[rows] - 2.0 * (zc[j, z] + r_left[j, 3] + r_right[j, 3])
        shares.append(push(p_hat.at[rows], p_hat.at[rows], partner))

    multiply(0)
    cross(0)
    forward("x", 3), forward("y", 3)
    begin(0)
    settle("x", 2), settle("x", 4)
    multiply(1)
    cross(1)
    travel(0, 2)
    multiply(3)
    cross(3)
    begin(1)
    travel(0, 3)
    for ring, item in (("y", 1), ("y", 2), ("y", 3), ("y", 4), ("x", 3)):
        settle(ring, item)
    begin(3)
    travel(0, 4)
    travel(1, 2)
    multiply(2)
    cross(2)
    half, tile = lax.rem(row, 2), lax.div(row, 2)

    def transposed(block):
        return f_all.at[pl.ds(pl.multiple_of(block * BLOCK + half * HALF, HALF), HALF), pl.ds(aligned(tile, HALF), HALF)]

    moves = [
        pltpu.make_async_remote_copy(
            src_ref=transposed(block), dst_ref=f_own.at[block], send_sem=send_sem.at[SEMAPHORES - 1 - block],
            recv_sem=recv_sem.at[SEMAPHORES - 1 - block], device_id=(col, row), device_id_type=MESH,
        )
        for block in range(3)
    ]
    stays = [pltpu.make_async_copy(transposed(block), f_own.at[block], local_sem.at[5 + block]) for block in range(3)]

    @pl.when(row != col)
    def _():
        for copy in moves:
            copy.start()

    @pl.when(row == col)
    def _():
        for copy in stays:
            copy.start()

    travel(3, 2)
    begin(2)
    travel(1, 3)
    travel(3, 3)
    travel(2, 2)
    grad_copy.wait_recv()
    own_rows = pl.ds(aligned(k, SUB), SUB)
    gt = gbuf[...].T
    cmat[:, 0:128] = gt
    for j in range(4):
        rows = pl.ds(pl.multiple_of(j * GROUP + k * SUB, 8), SUB)
        p_hat[rows] = cmat[rows, 0:128]
    arrive(0)
    travel(1, 4)
    travel(3, 4)
    travel(2, 3)
    arrive(1)
    arrive(3)
    travel(2, 4)
    local[4].wait()
    start_gradient(low, topv, cmat)
    arrive(2)
    for copy in shares:
        copy.wait_recv()

    @pl.when(row != col)
    def _():
        for copy in moves:
            copy.wait()

    @pl.when(row == col)
    def _():
        for copy in stays:
            copy.wait()

    for block in range(3):
        start = OFFSETS[block]
        rows = WIDTH - BLOCK * block
        wst[start : start + rows] = dot3(p_hat[BLOCK * block :], f_own[block], ((1,), (1,)))

    def scatter(src, unit, extent, reach, me, buffer):
        copies = []
        for d in range(1, extent):
            to = lax.rem(me + d, extent)
            copies.append(push(src(to), buffer.at[d - 1], reach(d)))
        return copies

    def total(own, copies, buffer):
        for d, copy in enumerate(copies):
            copy.wait_recv()
            own = own + buffer[d]
        return own

    def gather(ref, extent, reach):
        return [push(ref, ref, reach(d)) for d in range(1, extent)]

    def arrived(copies):
        for copy in copies:
            copy.wait_recv()

    def rows_of(base, start, size):
        return pl.ds(pl.multiple_of(base + start, 8), size)

    sc = scatter(lambda to: wst.at[rows_of(1024, to * 64, 64)], 64, NZ, at_z, z, r_c1)
    sa = scatter(lambda to: wst.at[rows_of(0, to * 128, 128)], 128, NX, at_x, x, r_a1)
    sb = scatter(lambda to: wst.at[rows_of(512, to * 128, 128)], 128, NY, at_y, y, r_b1)
    p_rows[...] = p_hat[...].T
    a1[...] = total(wst[rows_of(0, x * 128, 128)], sa, r_a1)
    sa = scatter(lambda to: a1.at[rows_of(0, to * 32, 32)], 32, NY, at_y, y, r_a2)
    b1[...] = total(wst[rows_of(512, y * 128, 128)], sb, r_b1)
    sb = scatter(lambda to: b1.at[rows_of(0, to * 32, 32)], 32, NX, at_x, x, r_b2)
    a2[z] = total(a1[rows_of(0, y * 32, 32)], sa, r_a2)
    sa = gather(a2.at[z], NZ, at_z)
    b2[z] = total(b1[rows_of(0, x * 32, 32)], sb, r_b2)
    sb = gather(b2.at[z], NZ, at_z)
    c1[...] = total(wst[rows_of(1024, z * 64, 64)], sc, r_c1)
    sc = scatter(lambda to: c1.at[rows_of(0, to * 16, 16)], 16, NX, at_x, x, r_c2)
    c2[y] = total(c1[rows_of(0, x * 16, 16)], sc, r_c2)
    sc = gather(c2.at[y], NY, at_y)
    inverse_transposed(inv, inv_t)
    arrived(sc)
    rows = rows_of(1024, z * 64 + x * 16, 16)
    wfull[k, rows] = c2[0] + c2[1] + c2[2] + c2[3]
    sc = gather(wfull.at[k, rows], NX, at_x)

    def over_z(ref):
        value = ref[0]
        for d in range(1, NZ):
            value = value + ref[d]
        return value

    arrived(sa)
    rows = rows_of(0, x * 128 + y * 32, 32)
    wfull[k, rows] = over_z(a2)
    sa = gather(wfull.at[k, rows], NY, at_y)
    arrived(sb)
    rows = rows_of(512, y * 128 + x * 32, 32)
    wfull[k, rows] = over_z(b2)
    sb = gather(wfull.at[k, rows], NX, at_x)
    arrived(sc)
    sc = gather(wfull.at[k, rows_of(1024, z * 64, 64)], NZ, at_z)
    arrived(sa)
    sa = gather(wfull.at[k, rows_of(0, x * 128, 128)], NX, at_x)
    arrived(sb)
    sb = gather(wfull.at[k, rows_of(512, y * 128, 128)], NY, at_y)
    out_rows[...] = dot6(p_rows[pl.ds(aligned(k, 64), 64)], inv[...])
    finals = []
    for start, copies in ((0, sa), (512, sb), (1024, sc)):
        arrived(copies)
        third = wfull.at[k, pl.ds(start, 512)]
        finals.append(push(third, third, partner))
    arrived(finals)
    finish_gradient(inv, inv_t, cmat, wfull, mmat, xmat, out_top)
    for copy in pending:
        copy.wait_send()


def inverse_diagonals(low, inv):
    rows, lanes = iota((HALF, HALF), 0), iota((HALF, HALF), 1)
    group = rows - lax.rem(rows, 8)

    @pl.loop(0, 6)
    def _(block):
        span = pl.ds(aligned(block, HALF), HALF)
        own = low[span, span]
        within = iota((16, 8, HALF), 1)
        value = jnp.where(rows == lanes, 1.0, 0.0).reshape(16, 8, HALF)
        for step in range(8):
            column = jnp.sum(jnp.where(lanes == group + step, own, 0.0), axis=1, keepdims=True)
            column = jnp.broadcast_to(column, (HALF, HALF)).reshape(16, 8, HALF)
            solved = value[:, step : step + 1] / column[:, step : step + 1]
            solved = jnp.broadcast_to(solved, (16, 8, HALF))
            value = jnp.where(within == step, solved, jnp.where(within > step, value - column * solved, value))
        value = value.reshape(HALF, HALF)
        for size in (8, 16, 32, 64):
            upper, left = lax.div(rows, size), lax.div(lanes, size)
            mask = jnp.logical_and(left + 1 == upper, lax.rem(upper, 2) == 1)
            value = value - dot6(value, dot6(jnp.where(mask, own, 0.0), value))
        inv[span, span] = value


def inverse_blocks(low, inv):
    zero = jnp.zeros((HALF, HALF), F32)
    for block in range(3):
        first, second = slice(block * BLOCK, block * BLOCK + HALF), slice(block * BLOCK + HALF, block * BLOCK + BLOCK)
        inv[second, first] = -dot6(inv[second, second], dot6(low[second, first], inv[first, first]))
        inv[first, second] = zero
    one, two, three = slice(0, BLOCK), slice(BLOCK, 2 * BLOCK), slice(2 * BLOCK, 3 * BLOCK)
    inv[two, one] = -dot6(inv[two, two], dot6(low[two, one], inv[one, one]))
    inv[three, two] = -dot6(inv[three, three], dot6(low[three, two], inv[two, two]))
    inv[three, one] = -dot6(
        inv[three, three], dot6(low[three, one], inv[one, one]) + dot6(low[three, two], inv[two, one])
    )
    inv[one, 256:768] = jnp.zeros((BLOCK, 512), F32)
    inv[two, 512:768] = jnp.zeros((BLOCK, BLOCK), F32)


def inverse_transposed(inv, inv_t):
    for i in range(3):
        for j in range(i, 3):
            rows, lanes = slice(BLOCK * i, BLOCK * i + BLOCK), slice(BLOCK * j, BLOCK * j + BLOCK)
            inv_t[rows, lanes] = inv[lanes, rows].T


def start_gradient(low, topv, cmat):
    rows, lanes = iota((BLOCK, BLOCK), 0), iota((BLOCK, BLOCK), 1)
    for i in range(3):
        block = slice(BLOCK * i, BLOCK * i + BLOCK)
        flipped = low[BLOCK * i :, block].T
        for j in range(3):
            other = slice(BLOCK * j, BLOCK * j + BLOCK)
            if j > i:
                cmat[block, other] = jnp.zeros((BLOCK, BLOCK), F32)
                continue
            value = dot3(flipped, topv[BLOCK * i :, other])
            if i == j:
                value = jnp.where(rows > lanes, value, jnp.where(rows == lanes, 0.5 * value, 0.0))
            cmat[block, other] = value


def finish_gradient(inv, inv_t, cmat, wfull, mmat, xmat, out_top):
    rows, lanes = iota((BLOCK, HALF), 0), iota((BLOCK, HALF), 1)
    for block in range(3):
        for side in range(2):
            start = OFFSETS[block]
            column = slice(BLOCK * block + HALF * side, BLOCK * block + HALF * side + HALF)
            value = wfull[side, start : start + BLOCK]
            place = lanes + HALF * side
            value = jnp.where(rows > place, value, jnp.where(rows == place, 0.5 * value, 0.0))
            cmat[BLOCK * block : BLOCK * block + BLOCK, column] -= value
            if block < 2:
                end = start + WIDTH - BLOCK * block
                cmat[BLOCK * block + BLOCK :, column] -= wfull[side, start + BLOCK : end]
    for i in range(3):
        block = slice(BLOCK * i, BLOCK * i + BLOCK)
        mmat[block] = dot3(inv_t[block, BLOCK * i :], cmat[BLOCK * i :])
    for j in range(3):
        block = slice(BLOCK * j, BLOCK * j + BLOCK)
        xmat[:, block] = dot3(mmat[:, BLOCK * j :], inv[BLOCK * j :, block])
    rows, lanes = iota((BLOCK, BLOCK), 0), iota((BLOCK, BLOCK), 1)
    for i in range(3):
        for j in range(3):
            block, other = slice(BLOCK * i, BLOCK * i + BLOCK), slice(BLOCK * j, BLOCK * j + BLOCK)
            if j > i:
                out_top[block, other] = jnp.zeros((BLOCK, BLOCK), F32)
                continue
            value = xmat[block, other] + xmat[other, block].T
            if i == j:
                value = jnp.where(rows > lanes, value, jnp.where(rows == lanes, 0.5 * value, 0.0))
            out_top[block, other] = value


def per_device(trail_grad, factor_rows, factor_top, rows_grad, top_grad):
    anywhere = pl.BlockSpec(memory_space=pl.ANY)
    inside = pl.BlockSpec(memory_space=pltpu.VMEM)
    square = pltpu.VMEM((WIDTH, WIDTH), F32)

    def vmem(*shape):
        return pltpu.VMEM(shape, F32)

    return pl.pallas_call(
        kernel,
        out_shape=(jax.ShapeDtypeStruct((64, WIDTH), F32), jax.ShapeDtypeStruct((WIDTH, WIDTH), F32)),
        in_specs=[anywhere] * 5,
        out_specs=(inside, inside),
        scratch_shapes=[
            vmem(1024, 1024), pltpu.VMEM((1024, 1024), BF16), pltpu.VMEM((1024, 1024), BF16),
            vmem(WIDTH, 1024), vmem(4, GROUP, 1024), vmem(4, SUB, 1024), vmem(4, 8, SUB, 128), vmem(4, 4, SUB, 128),
            vmem(4, 4, SUB, 128), square, square, square, square, square, square, square, vmem(128, WIDTH), vmem(WIDTH, 128),
            vmem(128, WIDTH), vmem(3, 128, 128), vmem(1536, 128), vmem(3, 128, 128), vmem(3, 32, 128), vmem(128, 128),
            vmem(8, 32, 128), vmem(3, 128, 128), vmem(3, 32, 128), vmem(128, 128), vmem(8, 32, 128), vmem(7, 64, 128),
            vmem(3, 16, 128), vmem(64, 128), vmem(4, 16, 128), vmem(2, 1536, 128), pltpu.SemaphoreType.DMA((8,)),
            pltpu.SemaphoreType.DMA((SEMAPHORES,)), pltpu.SemaphoreType.DMA((SEMAPHORES,)),
        ],
        compiler_params=pltpu.CompilerParams(collective_id=0, has_side_effects=True, vmem_limit_bytes=62 << 20),
    )(trail_grad, factor_rows.T, factor_top, rows_grad, top_grad)


def solution(mesh):
    placed = (P("row", "col"), P("col", "row"), P(), P(("row", "col"), None), P())
    return jax.shard_map(
        per_device,
        mesh=mesh,
        in_specs=placed,
        out_specs=(P(("row", "col"), None), P()),
        check_vma=False,
    )
```

```python
import jax
import jax.numpy as jnp
from jax import lax
from jax.experimental import pallas as pl
from jax.experimental.pallas import tpu as pltpu
from jax.sharding import PartitionSpec as P

MESH = pl.DeviceIdType.MESH
F32, BF16 = jnp.float32, jnp.bfloat16
HIGHEST = lax.Precision.HIGHEST
NX, NY, NZ = 4, 4, 8
BLOCK, HALF, WIDTH = 256, 128, 768
CHUNK, PIECE = 48, 24
GROUP, SUB = 192, 96
OFFSETS = (0, 768, 1280)
SEMAPHORES = 200


def contract(left, right, dims, precision=None):
    return lax.dot_general(left, right, (dims, ((), ())), precision=precision, preferred_element_type=F32)


def split(value):
    high = value.astype(BF16)
    return high, (value - high.astype(F32)).astype(BF16)


def dot3(left, right, dims=((1,), (0,))):
    left_high, left_low = split(left)
    right_high, right_low = split(right)
    return (
        contract(left_low, right_high, dims)
        + contract(left_high, right_low, dims)
        + contract(left_high, right_high, dims)
    )


def dot6(left, right):
    return contract(left, right, ((1,), (0,)), HIGHEST)


def iota(shape, dim):
    return lax.broadcasted_iota(jnp.int32, shape, dim)


def aligned(index, unit):
    return pl.multiple_of(index * unit, unit)


def kernel(trail, factor, lower, grad, top, out_rows, out_top, strail, s_high, s_low, f_all, zt, cx, zc, r_left, r_right, low, topv,
           inv, inv_t, cmat, mmat, xmat, gbuf, p_hat, p_rows, planes, f_here, wst, r_a1, r_a2, a1, a2, r_b1, r_b2, b1, b2, r_c1, r_c2, c1, c2,
           wfull, local_sem, send_sem, recv_sem):
    row, col = lax.axis_index("row"), lax.axis_index("col")
    y, x = lax.div(row, NX), lax.rem(row, NX)
    z, k = lax.div(col, 2), lax.rem(col, 2)
    other = 1 - k

    def at_x(d):
        return (y * NX + lax.rem(x + d + NX, NX), col)

    def at_y(d):
        return (lax.rem(y + d + NY, NY) * NX + x, col)

    def at_z(d):
        return (row, lax.rem(z + d + NZ, NZ) * 2 + k)

    partner = (row, z * 2 + other)
    count = [0]
    pending = []

    def push(src, dst, device):
        slot = count[0]
        count[0] += 1
        copy = pltpu.make_async_remote_copy(
            src_ref=src, dst_ref=dst, send_sem=send_sem.at[slot], recv_sem=recv_sem.at[slot], device_id=device, device_id_type=MESH
        )
        copy.start()
        pending.append(copy)
        return copy

    local = [
        pltpu.make_async_copy(factor, f_all.at[pl.ds(aligned(row, CHUNK), CHUNK)], local_sem.at[0]),
        pltpu.make_async_copy(grad, gbuf.at[pl.ds(aligned(k, 64), 64)], local_sem.at[1]),
        pltpu.make_async_copy(trail, strail, local_sem.at[2]),
        pltpu.make_async_copy(lower, low, local_sem.at[3]),
        pltpu.make_async_copy(top, topv, local_sem.at[4]),
    ]
    for copy in local:
        copy.start()

    barrier = pltpu.get_barrier_semaphore()

    def greet(device):
        pl.semaphore_signal(barrier, inc=1, device_id=device, device_id_type=MESH)

    for d in range(1, NX * NY):
        greet((lax.rem(row + d, NX * NY), col))
    for d in range(1, NZ):
        greet(at_z(d))
    greet(partner)
    pl.semaphore_wait(barrier, NX * NY + NZ - 1)

    local[0].wait()
    local[1].wait()

    rings = {"x": at_x, "y": at_y}

    def piece(ring, item, shift):
        if ring == "x":
            owner_x, owner_y = lax.rem(x + shift + NX, NX), y if item == 0 else lax.rem(y + item - 1, NY)
            offset = 0 if item == 0 else PIECE
        else:
            owner_y, owner_x = lax.rem(y + shift + NY, NY), x if item == 0 else lax.rem(x + item - 1, NX)
            offset = PIECE if item == 0 else 0
        return pl.ds(pl.multiple_of((owner_y * NX + owner_x) * CHUNK + offset, 8), PIECE)

    full, halves = {}, {}

    def send(ring, item):
        rows = f_all.at[piece(ring, item, 0)]
        full[ring, item] = [push(rows, rows, rings[ring](1)), push(rows, rows, rings[ring](-1))]

    def forward(ring, item):
        from_left, from_right = full[ring, item]
        from_left.wait_recv()
        rows = f_all.at[piece(ring, item, -1), pl.ds(0, 512)]
        right = push(rows, rows, rings[ring](1))
        from_right.wait_recv()
        rows = f_all.at[piece(ring, item, 1), pl.ds(512, 512)]
        halves[ring, item] = [right, push(rows, rows, rings[ring](-1))]

    def settle(ring, item):
        for copy in halves[ring, item]:
            copy.wait_recv()

    send("x", 0), send("y", 0), send("x", 1), send("y", 1)
    own_half = pl.ds(aligned(k, 64), 64)
    grad_copy = push(gbuf.at[own_half], gbuf.at[own_half], partner)
    chunk = pl.ds(aligned(row, CHUNK), CHUNK)
    spread = []
    for d in range(1, NZ):
        lanes = pl.ds(aligned(lax.rem(z + d, NZ), 128), 128)
        spread.append(push(f_all.at[chunk, lanes], planes.at[z], at_z(d)))
    keep = pltpu.make_async_copy(f_all.at[chunk, pl.ds(aligned(z, 128), 128)], planes.at[z], local_sem.at[5])
    keep.start()
    owner = lax.rem(row, 2) == k
    landing = f_here.at[chunk]
    pair = lax.div(row, 2)
    exchange, first_move, first_stay = [], [], []

    def rearrange():
        keep.wait()
        for copy in spread:
            copy.wait_recv()
        for d in range(NZ):
            block = lax.rem(pair + d, NZ)
            copy = pltpu.make_async_remote_copy(
                src_ref=planes.at[block], dst_ref=landing, send_sem=send_sem.at[SEMAPHORES - 2 - d],
                recv_sem=recv_sem.at[SEMAPHORES - 1], device_id=(block * 2 + k, col), device_id_type=MESH,
            )
            if d == 0:
                first_move.append(copy)
                first_stay.append(pltpu.make_async_copy(planes.at[block], landing, local_sem.at[6]))
            else:
                copy.start()
                exchange.append(copy)

        @pl.when(jnp.logical_not(owner))
        def _():
            first_move[0].start()

        @pl.when(owner)
        def _():
            first_stay[0].start()

    share = pltpu.make_async_remote_copy(
        src_ref=f_here, dst_ref=f_here, send_sem=send_sem.at[SEMAPHORES - 10], recv_sem=recv_sem.at[SEMAPHORES - 10],
        device_id=partner, device_id_type=MESH,
    )

    def pass_on():
        for copy in exchange:
            copy.wait_send()

        @pl.when(owner)
        def _():
            most = f_here.at[0 : WIDTH - CHUNK]
            pltpu.make_async_remote_copy(
                src_ref=most, dst_ref=most, send_sem=send_sem.at[SEMAPHORES - 1], recv_sem=recv_sem.at[SEMAPHORES - 1],
                device_id=partner, device_id_type=MESH,
            ).wait_recv()
            first_stay[0].wait()
            share.start()

        @pl.when(jnp.logical_not(owner))
        def _():
            first_move[0].wait_send()

    def passed():
        @pl.when(owner)
        def _():
            share.wait_send()

        @pl.when(jnp.logical_not(owner))
        def _():
            share.wait_recv()

    local[2].wait()

    @pl.loop(0, 8)
    def _(step):
        rows = pl.ds(aligned(step, 128), 128)
        s_high[rows], s_low[rows] = split(strail[rows])

    forward("x", 0), forward("y", 0)
    send("x", 2), send("y", 2), send("x", 4), send("y", 4)
    local[3].wait()
    inverse_pair(low, inv, 0)
    forward("x", 1), forward("y", 1)
    settle("x", 0), settle("y", 0)
    send("x", 3), send("y", 3)
    inverse_pair(low, inv, 1)
    forward("x", 2), forward("y", 2), forward("x", 4), forward("y", 4)
    grad_copy.wait_recv()
    cmat[:, 0:128] = gbuf[...].T
    for j in range(4):
        rows = pl.ds(pl.multiple_of(j * GROUP + k * SUB, 8), SUB)
        p_hat[rows] = cmat[rows, 0:128]
    settle("x", 1)

    def multiply(j):
        rows = pl.ds(aligned(lax.rem(y + j, NY), GROUP), GROUP)
        f_high, f_low = split(f_all[rows])

        @pl.loop(0, 4)
        def _(step):
            part = pl.ds(aligned(step, BLOCK), BLOCK)
            dims = ((1,), (1,))
            zt[j, :, part] = (
                contract(f_low, s_high[part], dims) + contract(f_high, s_low[part], dims) + contract(f_high, s_high[part], dims)
            )

    crossing = {}

    def cross(j):
        crossing[j] = push(zt.at[j, pl.ds(aligned(other, SUB), SUB)], cx.at[j], partner)

    lefts, rights = {}, {}

    def begin(j):
        crossing[j].wait_recv()
        own = pl.ds(aligned(k, SUB), SUB)
        for d in range(NZ):
            lanes = pl.ds(128 * d, 128)
            zc[j, d] = zt[j, own, lanes] + cx[j, :, lanes]
        far = lax.rem(z + 4, NZ)
        lefts[j] = push(zc.at[j, far, pl.ds(0, 48)], r_left.at[j, 0, pl.ds(0, 48)], at_z(-1))
        rights[j] = push(zc.at[j, far, pl.ds(48, 48)], r_right.at[j, 0, pl.ds(48, 48)], at_z(1))

    def travel(j, step):
        to_left, to_right = lax.rem(z + 3 + step, NZ), lax.rem(z + 5 - step, NZ)
        lefts[j].wait_recv()
        if step == 2:
            zc[j, to_left, 0:48] += r_left[j, 0, 0:48]
        else:
            zc[j, to_left] += r_left[j, step - 2]
        lefts[j] = push(zc.at[j, to_left], r_left.at[j, step - 1], at_z(-1))
        rights[j].wait_recv()
        if step == 2:
            zc[j, to_right, 48:96] += r_right[j, 0, 48:96]
        else:
            zc[j, to_right] += r_right[j, step - 2]
        rights[j] = push(zc.at[j, to_right], r_right.at[j, step - 1], at_z(1))

    shares = []

    def arrive(j):
        lefts[j].wait_recv()
        rights[j].wait_recv()
        rows = pl.ds(pl.multiple_of(lax.rem(y + j, NY) * GROUP + k * SUB, 8), SUB)
        p_hat[rows] = p_hat[rows] - 2.0 * (zc[j, z] + r_left[j, 3] + r_right[j, 3])
        shares.append(push(p_hat.at[rows], p_hat.at[rows], partner))

    multiply(0)
    cross(0)
    forward("x", 3), forward("y", 3)
    rearrange()
    begin(0)
    settle("x", 2), settle("x", 4)
    multiply(1)
    cross(1)
    travel(0, 2)
    multiply(3)
    cross(3)
    begin(1)
    travel(0, 3)
    for ring, item in (("y", 1), ("y", 2), ("y", 3), ("y", 4), ("x", 3)):
        settle(ring, item)
    multiply(2)
    cross(2)
    begin(3)
    travel(0, 4)
    travel(1, 2)
    pass_on()
    begin(2)
    travel(3, 2)
    travel(1, 3)
    travel(2, 2)
    arrive(0)
    travel(3, 3)
    travel(1, 4)
    travel(2, 3)
    inverse_pair(low, inv, 2)
    arrive(1)
    travel(3, 4)
    travel(2, 4)
    arrive(3)
    local[4].wait()
    start_gradient(low, topv, cmat)
    arrive(2)
    for copy in shares:
        copy.wait_recv()
    passed()

    for block in range(3):
        start = OFFSETS[block]
        rows = WIDTH - BLOCK * block
        wst[start : start + rows] = dot3(p_hat[BLOCK * block :], f_here[pl.ds(pl.multiple_of(block * BLOCK + k * HALF, HALF), HALF)], ((1,), (1,)))

    def scatter(src, unit, extent, reach, me, buffer):
        copies = []
        for d in range(1, extent):
            to = lax.rem(me + d, extent)
            copies.append(push(src(to), buffer.at[d - 1], reach(d)))
        return copies

    def total(own, copies, buffer):
        for d, copy in enumerate(copies):
            copy.wait_recv()
            own = own + buffer[d]
        return own

    def gather(ref, extent, reach):
        return [push(ref, ref, reach(d)) for d in range(1, extent)]

    def arrived(copies):
        for copy in copies:
            copy.wait_recv()

    def rows_of(base, start, size):
        return pl.ds(pl.multiple_of(base + start, 8), size)

    sc = scatter(lambda to: wst.at[rows_of(1024, to * 64, 64)], 64, NZ, at_z, z, r_c1)
    sa = scatter(lambda to: wst.at[rows_of(0, to * 128, 128)], 128, NX, at_x, x, r_a1)
    sb = scatter(lambda to: wst.at[rows_of(512, to * 128, 128)], 128, NY, at_y, y, r_b1)
    p_rows[...] = p_hat[...].T
    a1[...] = total(wst[rows_of(0, x * 128, 128)], sa, r_a1)
    sa = scatter(lambda to: a1.at[rows_of(0, to * 32, 32)], 32, NY, at_y, y, r_a2)
    b1[...] = total(wst[rows_of(512, y * 128, 128)], sb, r_b1)
    sb = scatter(lambda to: b1.at[rows_of(0, to * 32, 32)], 32, NX, at_x, x, r_b2)
    a2[z] = total(a1[rows_of(0, y * 32, 32)], sa, r_a2)
    sa = gather(a2.at[z], NZ, at_z)
    b2[z] = total(b1[rows_of(0, x * 32, 32)], sb, r_b2)
    sb = gather(b2.at[z], NZ, at_z)
    c1[...] = total(wst[rows_of(1024, z * 64, 64)], sc, r_c1)
    sc = scatter(lambda to: c1.at[rows_of(0, to * 16, 16)], 16, NX, at_x, x, r_c2)
    c2[y] = total(c1[rows_of(0, x * 16, 16)], sc, r_c2)
    sc = gather(c2.at[y], NY, at_y)
    inverse_blocks(low, inv)
    inverse_transposed(inv, inv_t)
    arrived(sc)
    rows = rows_of(1024, z * 64 + x * 16, 16)
    wfull[k, rows] = c2[0] + c2[1] + c2[2] + c2[3]
    sc = gather(wfull.at[k, rows], NX, at_x)

    def over_z(ref):
        value = ref[0]
        for d in range(1, NZ):
            value = value + ref[d]
        return value

    arrived(sa)
    rows = rows_of(0, x * 128 + y * 32, 32)
    wfull[k, rows] = over_z(a2)
    sa = gather(wfull.at[k, rows], NY, at_y)
    arrived(sb)
    rows = rows_of(512, y * 128 + x * 32, 32)
    wfull[k, rows] = over_z(b2)
    sb = gather(wfull.at[k, rows], NX, at_x)
    arrived(sc)
    sc = gather(wfull.at[k, rows_of(1024, z * 64, 64)], NZ, at_z)
    arrived(sa)
    sa = gather(wfull.at[k, rows_of(0, x * 128, 128)], NX, at_x)
    arrived(sb)
    sb = gather(wfull.at[k, rows_of(512, y * 128, 128)], NY, at_y)
    out_rows[...] = dot6(p_rows[pl.ds(aligned(k, 64), 64)], inv[...])
    finals = []
    for start, copies in ((0, sa), (512, sb), (1024, sc)):
        arrived(copies)
        third = wfull.at[k, pl.ds(start, 512)]
        finals.append(push(third, third, partner))
    arrived(finals)
    finish_gradient(inv, inv_t, cmat, wfull, mmat, xmat, out_top)
    for copy in pending:
        copy.wait_send()


def odd(value, size):
    return value.reshape(HALF // (2 * size), 2, size, HALF)[:, 1].reshape(HALF // 2, HALF)


def inverse_pair(low, inv, which):
    rows, lanes = iota((HALF, HALF), 0), iota((HALF, HALF), 1)
    group = rows - lax.rem(rows, 8)
    within = iota((16, 8, HALF), 1)
    spans = [slice(which * BLOCK + HALF * i, which * BLOCK + HALF * i + HALF) for i in range(2)]
    owns = [low[span, span] for span in spans]
    values = [jnp.where(rows == lanes, 1.0, 0.0).reshape(16, 8, HALF)] * 2
    for step in range(8):
        for i in range(2):
            value = values[i]
            column = jnp.sum(jnp.where(lanes == group + step, owns[i], 0.0), axis=1, keepdims=True)
            column = jnp.broadcast_to(column, (HALF, HALF)).reshape(16, 8, HALF)
            solved = value[:, step : step + 1] / column[:, step : step + 1]
            solved = jnp.broadcast_to(solved, (16, 8, HALF))
            values[i] = jnp.where(within == step, solved, jnp.where(within > step, value - column * solved, value))
    values = [value.reshape(HALF, HALF) for value in values]
    for size in (8, 16, 32, 64):
        upper, left = lax.div(rows, size), lax.div(lanes, size)
        mask = jnp.logical_and(left + 1 == upper, lax.rem(upper, 2) == 1)
        inner = [dot6(odd(jnp.where(mask, owns[i], 0.0), size), values[i]) for i in range(2)]
        shape = (HALF // (2 * size), 1, size, HALF)
        none = jnp.zeros(shape, F32)
        inner = [jnp.concatenate([none, value.reshape(shape)], axis=1).reshape(HALF, HALF) for value in inner]
        inner = [dot6(odd(values[i], size), inner[i]) for i in range(2)]
        inner = [jnp.concatenate([none, value.reshape(shape)], axis=1).reshape(HALF, HALF) for value in inner]
        values = [values[i] - inner[i] for i in range(2)]
    first, second = spans
    inv[first, first] = values[0]
    inv[second, second] = values[1]
    inv[second, first] = -dot6(values[1], dot6(low[second, first], values[0]))
    inv[first, second] = jnp.zeros((HALF, HALF), F32)


def inverse_blocks(low, inv):
    one, two, three = slice(0, BLOCK), slice(BLOCK, 2 * BLOCK), slice(2 * BLOCK, 3 * BLOCK)
    inv[two, one] = -dot6(inv[two, two], dot6(low[two, one], inv[one, one]))
    inv[three, two] = -dot6(inv[three, three], dot6(low[three, two], inv[two, two]))
    inv[three, one] = -dot6(
        inv[three, three], dot6(low[three, one], inv[one, one]) + dot6(low[three, two], inv[two, one])
    )
    inv[one, 256:768] = jnp.zeros((BLOCK, 512), F32)
    inv[two, 512:768] = jnp.zeros((BLOCK, BLOCK), F32)


def inverse_transposed(inv, inv_t):
    for i in range(3):
        for j in range(i, 3):
            rows, lanes = slice(BLOCK * i, BLOCK * i + BLOCK), slice(BLOCK * j, BLOCK * j + BLOCK)
            inv_t[rows, lanes] = inv[lanes, rows].T


def start_gradient(low, topv, cmat):
    rows, lanes = iota((BLOCK, BLOCK), 0), iota((BLOCK, BLOCK), 1)
    for i in range(3):
        block = slice(BLOCK * i, BLOCK * i + BLOCK)
        flipped = low[BLOCK * i :, block].T
        for j in range(3):
            other = slice(BLOCK * j, BLOCK * j + BLOCK)
            if j > i:
                cmat[block, other] = jnp.zeros((BLOCK, BLOCK), F32)
                continue
            value = dot3(flipped, topv[BLOCK * i :, other])
            if i == j:
                value = jnp.where(rows > lanes, value, jnp.where(rows == lanes, 0.5 * value, 0.0))
            cmat[block, other] = value


def finish_gradient(inv, inv_t, cmat, wfull, mmat, xmat, out_top):
    rows, lanes = iota((BLOCK, HALF), 0), iota((BLOCK, HALF), 1)
    for block in range(3):
        for side in range(2):
            start = OFFSETS[block]
            column = slice(BLOCK * block + HALF * side, BLOCK * block + HALF * side + HALF)
            value = wfull[side, start : start + BLOCK]
            place = lanes + HALF * side
            value = jnp.where(rows > place, value, jnp.where(rows == place, 0.5 * value, 0.0))
            cmat[BLOCK * block : BLOCK * block + BLOCK, column] -= value
            if block < 2:
                end = start + WIDTH - BLOCK * block
                cmat[BLOCK * block + BLOCK :, column] -= wfull[side, start + BLOCK : end]
    for i in range(3):
        block = slice(BLOCK * i, BLOCK * i + BLOCK)
        mmat[block] = dot3(inv_t[block, BLOCK * i :], cmat[BLOCK * i :])
    for j in range(3):
        block = slice(BLOCK * j, BLOCK * j + BLOCK)
        xmat[:, block] = dot3(mmat[:, BLOCK * j :], inv[BLOCK * j :, block])
    rows, lanes = iota((BLOCK, BLOCK), 0), iota((BLOCK, BLOCK), 1)
    for i in range(3):
        for j in range(3):
            block, other = slice(BLOCK * i, BLOCK * i + BLOCK), slice(BLOCK * j, BLOCK * j + BLOCK)
            if j > i:
                out_top[block, other] = jnp.zeros((BLOCK, BLOCK), F32)
                continue
            value = xmat[block, other] + xmat[other, block].T
            if i == j:
                value = jnp.where(rows > lanes, value, jnp.where(rows == lanes, 0.5 * value, 0.0))
            out_top[block, other] = value


def per_device(trail_grad, factor_rows, factor_top, rows_grad, top_grad):
    anywhere = pl.BlockSpec(memory_space=pl.ANY)
    inside = pl.BlockSpec(memory_space=pltpu.VMEM)
    square = pltpu.VMEM((WIDTH, WIDTH), F32)

    def vmem(*shape):
        return pltpu.VMEM(shape, F32)

    return pl.pallas_call(
        kernel,
        out_shape=(jax.ShapeDtypeStruct((64, WIDTH), F32), jax.ShapeDtypeStruct((WIDTH, WIDTH), F32)),
        in_specs=[anywhere] * 5,
        out_specs=(inside, inside),
        scratch_shapes=[
            vmem(1024, 1024), pltpu.VMEM((1024, 1024), BF16), pltpu.VMEM((1024, 1024), BF16),
            vmem(WIDTH, 1024), vmem(4, GROUP, 1024), vmem(4, SUB, 1024), vmem(4, 8, SUB, 128), vmem(4, 4, SUB, 128),
            vmem(4, 4, SUB, 128), square, square, square, square, square, square, square, vmem(128, WIDTH), vmem(WIDTH, 128),
            vmem(128, WIDTH), vmem(NZ, CHUNK, 128), vmem(WIDTH, 128), vmem(1536, 128), vmem(3, 128, 128), vmem(3, 32, 128), vmem(128, 128),
            vmem(8, 32, 128), vmem(3, 128, 128), vmem(3, 32, 128), vmem(128, 128), vmem(8, 32, 128), vmem(7, 64, 128),
            vmem(3, 16, 128), vmem(64, 128), vmem(4, 16, 128), vmem(2, 1536, 128), pltpu.SemaphoreType.DMA((8,)),
            pltpu.SemaphoreType.DMA((SEMAPHORES,)), pltpu.SemaphoreType.DMA((SEMAPHORES,)),
        ],
        compiler_params=pltpu.CompilerParams(collective_id=0, has_side_effects=True, vmem_limit_bytes=62 << 20),
    )(trail_grad, factor_rows.T, factor_top, rows_grad, top_grad)


def solution(mesh):
    placed = (P("row", "col"), P("col", "row"), P(), P(("row", "col"), None), P())
    return jax.shard_map(
        per_device,
        mesh=mesh,
        in_specs=placed,
        out_specs=(P(("row", "col"), None), P()),
        check_vma=False,
    )
```

```python
import jax
import jax.numpy as jnp
from jax import lax
from jax.experimental import pallas as pl
from jax.experimental.pallas import tpu as pltpu
from jax.sharding import PartitionSpec as P

MESH = pl.DeviceIdType.MESH
F32, BF16 = jnp.float32, jnp.bfloat16
HIGHEST = lax.Precision.HIGHEST
NX, NY, NZ = 4, 4, 8
BLOCK, HALF, WIDTH = 256, 128, 768
CHUNK, PIECE = 48, 24
GROUP, SUB = 192, 96
OFFSETS = (0, 768, 1280)
SEMAPHORES = 200


def contract(left, right, dims, precision=None):
    return lax.dot_general(left, right, (dims, ((), ())), precision=precision, preferred_element_type=F32)


def split(value):
    high = value.astype(BF16)
    return high, (value - high.astype(F32)).astype(BF16)


def dot3(left, right, dims=((1,), (0,))):
    left_high, left_low = split(left)
    right_high, right_low = split(right)
    return (
        contract(left_low, right_high, dims)
        + contract(left_high, right_low, dims)
        + contract(left_high, right_high, dims)
    )


def dot6(left, right):
    return contract(left, right, ((1,), (0,)), HIGHEST)


def iota(shape, dim):
    return lax.broadcasted_iota(jnp.int32, shape, dim)


def aligned(index, unit):
    return pl.multiple_of(index * unit, unit)


def kernel(trail, factor, lower, grad, top, out_rows, out_top, strail, s_high, s_low, f_all, zt, cx, zc, r_left, r_right, low, topv,
           inv, i_high, i_low, t_high, t_low, cmat, m_high, m_low, xmat, gbuf, p_hat, p_rows, planes, f_here, wst, r_a1, r_a2, a1, a2, r_b1, r_b2, b1, b2, r_c1, r_c2, c1, c2,
           wfull, local_sem, send_sem, recv_sem):
    row, col = lax.axis_index("row"), lax.axis_index("col")
    y, x = lax.div(row, NX), lax.rem(row, NX)
    z, k = lax.div(col, 2), lax.rem(col, 2)
    other = 1 - k

    def at_x(d):
        return (y * NX + lax.rem(x + d + NX, NX), col)

    def at_y(d):
        return (lax.rem(y + d + NY, NY) * NX + x, col)

    def at_z(d):
        return (row, lax.rem(z + d + NZ, NZ) * 2 + k)

    partner = (row, z * 2 + other)
    count = [0]
    pending = []

    def push(src, dst, device):
        slot = count[0]
        count[0] += 1
        copy = pltpu.make_async_remote_copy(
            src_ref=src, dst_ref=dst, send_sem=send_sem.at[slot], recv_sem=recv_sem.at[slot], device_id=device, device_id_type=MESH
        )
        copy.start()
        pending.append(copy)
        return copy

    local = [
        pltpu.make_async_copy(factor, f_all.at[pl.ds(aligned(row, CHUNK), CHUNK)], local_sem.at[0]),
        pltpu.make_async_copy(grad, gbuf.at[pl.ds(aligned(k, 64), 64)], local_sem.at[1]),
        pltpu.make_async_copy(trail, strail, local_sem.at[2]),
        pltpu.make_async_copy(lower, low, local_sem.at[3]),
        pltpu.make_async_copy(top, topv, local_sem.at[4]),
    ]
    for copy in local:
        copy.start()

    barrier = pltpu.get_barrier_semaphore()

    def greet(device):
        pl.semaphore_signal(barrier, inc=1, device_id=device, device_id_type=MESH)

    for d in range(1, NX * NY):
        greet((lax.rem(row + d, NX * NY), col))
    for d in range(1, NZ):
        greet(at_z(d))
    greet(partner)
    pl.semaphore_wait(barrier, NX * NY + NZ - 1)

    local[0].wait()
    local[1].wait()

    rings = {"x": at_x, "y": at_y}

    def piece(ring, item, shift):
        if ring == "x":
            owner_x, owner_y = lax.rem(x + shift + NX, NX), y if item == 0 else lax.rem(y + item - 1, NY)
            offset = 0 if item == 0 else PIECE
        else:
            owner_y, owner_x = lax.rem(y + shift + NY, NY), x if item == 0 else lax.rem(x + item - 1, NX)
            offset = PIECE if item == 0 else 0
        return pl.ds(pl.multiple_of((owner_y * NX + owner_x) * CHUNK + offset, 8), PIECE)

    full, halves = {}, {}

    def send(ring, item):
        rows = f_all.at[piece(ring, item, 0)]
        full[ring, item] = [push(rows, rows, rings[ring](1)), push(rows, rows, rings[ring](-1))]

    def forward(ring, item):
        from_left, from_right = full[ring, item]
        from_left.wait_recv()
        rows = f_all.at[piece(ring, item, -1), pl.ds(0, 512)]
        right = push(rows, rows, rings[ring](1))
        from_right.wait_recv()
        rows = f_all.at[piece(ring, item, 1), pl.ds(512, 512)]
        halves[ring, item] = [right, push(rows, rows, rings[ring](-1))]

    def settle(ring, item):
        for copy in halves[ring, item]:
            copy.wait_recv()

    send("x", 0), send("y", 0), send("x", 1), send("y", 1)
    own_half = pl.ds(aligned(k, 64), 64)
    grad_copy = push(gbuf.at[own_half], gbuf.at[own_half], partner)
    chunk = pl.ds(aligned(row, CHUNK), CHUNK)
    spread = []
    for d in range(1, NZ):
        lanes = pl.ds(aligned(lax.rem(z + d, NZ), 128), 128)
        spread.append(push(f_all.at[chunk, lanes], planes.at[z], at_z(d)))
    keep = pltpu.make_async_copy(f_all.at[chunk, pl.ds(aligned(z, 128), 128)], planes.at[z], local_sem.at[5])
    keep.start()
    owner = lax.rem(row, 2) == k
    landing = f_here.at[chunk]
    pair = lax.div(row, 2)
    exchange, first_move, first_stay = [], [], []

    def rearrange():
        keep.wait()
        for copy in spread:
            copy.wait_recv()
        for d in range(NZ):
            block = lax.rem(pair + d, NZ)
            copy = pltpu.make_async_remote_copy(
                src_ref=planes.at[block], dst_ref=landing, send_sem=send_sem.at[SEMAPHORES - 2 - d],
                recv_sem=recv_sem.at[SEMAPHORES - 1], device_id=(block * 2 + k, col), device_id_type=MESH,
            )
            if d == 0:
                first_move.append(copy)
                first_stay.append(pltpu.make_async_copy(planes.at[block], landing, local_sem.at[6]))
            else:
                copy.start()
                exchange.append(copy)

        @pl.when(jnp.logical_not(owner))
        def _():
            first_move[0].start()

        @pl.when(owner)
        def _():
            first_stay[0].start()

    share = pltpu.make_async_remote_copy(
        src_ref=f_here, dst_ref=f_here, send_sem=send_sem.at[SEMAPHORES - 10], recv_sem=recv_sem.at[SEMAPHORES - 10],
        device_id=partner, device_id_type=MESH,
    )

    def pass_on():
        for copy in exchange:
            copy.wait_send()

        @pl.when(owner)
        def _():
            most = f_here.at[0 : WIDTH - CHUNK]
            pltpu.make_async_remote_copy(
                src_ref=most, dst_ref=most, send_sem=send_sem.at[SEMAPHORES - 1], recv_sem=recv_sem.at[SEMAPHORES - 1],
                device_id=partner, device_id_type=MESH,
            ).wait_recv()
            first_stay[0].wait()
            share.start()

        @pl.when(jnp.logical_not(owner))
        def _():
            first_move[0].wait_send()

    def passed():
        @pl.when(owner)
        def _():
            share.wait_send()

        @pl.when(jnp.logical_not(owner))
        def _():
            share.wait_recv()

    local[2].wait()

    @pl.loop(0, 8)
    def _(step):
        rows = pl.ds(aligned(step, 128), 128)
        s_high[rows], s_low[rows] = split(strail[rows])

    forward("x", 0), forward("y", 0)
    send("x", 2), send("y", 2)
    forward("x", 1), forward("y", 1)
    send("x", 4), send("y", 4)
    settle("x", 0), settle("y", 0)
    send("x", 3), send("y", 3)
    local[3].wait()
    inverse_pair(low, inv, 0)
    grad_copy.wait_recv()
    cmat[:, 0:128] = gbuf[...].T
    for j in range(4):
        rows = pl.ds(pl.multiple_of(j * GROUP + k * SUB, 8), SUB)
        p_hat[rows] = cmat[rows, 0:128]
    settle("x", 1)

    def multiply(*groups):
        parts = [split(f_all[pl.ds(aligned(lax.rem(y + j, NY), GROUP), GROUP)]) for j in groups]
        high = jnp.concatenate([part[0] for part in parts], axis=0)
        both = jnp.concatenate([part[0] for part in parts] + [part[1] for part in parts], axis=0)
        size = GROUP * len(groups)

        @pl.loop(0, 4)
        def _(step):
            part = pl.ds(aligned(step, BLOCK), BLOCK)
            dims = ((1,), (1,))
            first = contract(both, s_high[part], dims)
            value = first[:size] + first[size:] + contract(high, s_low[part], dims)
            for i, j in enumerate(groups):
                zt[j, :, part] = value[GROUP * i : GROUP * i + GROUP]

    crossing = {}

    def cross(j):
        crossing[j] = push(zt.at[j, pl.ds(aligned(other, SUB), SUB)], cx.at[j], partner)

    lefts, rights = {}, {}

    def begin(j):
        crossing[j].wait_recv()
        own = pl.ds(aligned(k, SUB), SUB)
        for d in range(NZ):
            lanes = pl.ds(128 * d, 128)
            zc[j, d] = zt[j, own, lanes] + cx[j, :, lanes]
        far = lax.rem(z + 4, NZ)
        lefts[j] = push(zc.at[j, far, pl.ds(0, 48)], r_left.at[j, 0, pl.ds(0, 48)], at_z(-1))
        rights[j] = push(zc.at[j, far, pl.ds(48, 48)], r_right.at[j, 0, pl.ds(48, 48)], at_z(1))

    def travel(j, step):
        to_left, to_right = lax.rem(z + 3 + step, NZ), lax.rem(z + 5 - step, NZ)
        lefts[j].wait_recv()
        if step == 2:
            zc[j, to_left, 0:48] += r_left[j, 0, 0:48]
        else:
            zc[j, to_left] += r_left[j, step - 2]
        lefts[j] = push(zc.at[j, to_left], r_left.at[j, step - 1], at_z(-1))
        rights[j].wait_recv()
        if step == 2:
            zc[j, to_right, 48:96] += r_right[j, 0, 48:96]
        else:
            zc[j, to_right] += r_right[j, step - 2]
        rights[j] = push(zc.at[j, to_right], r_right.at[j, step - 1], at_z(1))

    shares = []

    def arrive(j):
        lefts[j].wait_recv()
        rights[j].wait_recv()
        rows = pl.ds(pl.multiple_of(lax.rem(y + j, NY) * GROUP + k * SUB, 8), SUB)
        p_hat[rows] = p_hat[rows] - 2.0 * (zc[j, z] + r_left[j, 3] + r_right[j, 3])
        shares.append(push(p_hat.at[rows], p_hat.at[rows], partner))

    multiply(0)
    cross(0)
    forward("x", 2), forward("y", 2), forward("x", 4), forward("y", 4)
    rearrange()
    begin(0)
    forward("x", 3), forward("y", 3)
    travel(0, 2)
    settle("x", 2), settle("x", 4)
    multiply(1, 3)
    cross(1)
    cross(3)
    travel(0, 3)
    for ring, item in (("y", 1), ("y", 2), ("y", 3), ("y", 4), ("x", 3)):
        settle(ring, item)
    multiply(2)
    cross(2)
    travel(0, 4)
    begin(1)
    begin(3)
    pass_on()
    begin(2)
    travel(1, 2)
    travel(3, 2)
    arrive(0)
    travel(2, 2)
    inverse_pair(low, inv, 1)
    travel(1, 3)
    travel(3, 3)
    travel(2, 3)
    inverse_pair(low, inv, 2)
    travel(1, 4)
    travel(3, 4)
    travel(2, 4)
    local[4].wait()
    start_gradient(low, topv, cmat)
    arrive(1)
    arrive(3)
    arrive(2)
    for copy in shares:
        copy.wait_recv()
    passed()

    for block in range(3):
        start = OFFSETS[block]
        rows = WIDTH - BLOCK * block
        wst[start : start + rows] = dot3(p_hat[BLOCK * block :], f_here[pl.ds(pl.multiple_of(block * BLOCK + k * HALF, HALF), HALF)], ((1,), (1,)))

    def scatter(src, unit, extent, reach, me, buffer):
        copies = []
        for d in range(1, extent):
            to = lax.rem(me + d, extent)
            copies.append(push(src(to), buffer.at[d - 1], reach(d)))
        return copies

    def total(own, copies, buffer):
        for d, copy in enumerate(copies):
            copy.wait_recv()
            own = own + buffer[d]
        return own

    def gather(ref, extent, reach):
        return [push(ref, ref, reach(d)) for d in range(1, extent)]

    def arrived(copies):
        for copy in copies:
            copy.wait_recv()

    def rows_of(base, start, size):
        return pl.ds(pl.multiple_of(base + start, 8), size)

    sc = scatter(lambda to: wst.at[rows_of(1024, to * 64, 64)], 64, NZ, at_z, z, r_c1)
    sa = scatter(lambda to: wst.at[rows_of(0, to * 128, 128)], 128, NX, at_x, x, r_a1)
    sb = scatter(lambda to: wst.at[rows_of(512, to * 128, 128)], 128, NY, at_y, y, r_b1)
    p_rows[...] = p_hat[...].T
    inverse_blocks(low, inv)
    a1[...] = total(wst[rows_of(0, x * 128, 128)], sa, r_a1)
    sa = scatter(lambda to: a1.at[rows_of(0, to * 32, 32)], 32, NY, at_y, y, r_a2)
    b1[...] = total(wst[rows_of(512, y * 128, 128)], sb, r_b1)
    sb = scatter(lambda to: b1.at[rows_of(0, to * 32, 32)], 32, NX, at_x, x, r_b2)
    inverse_halves(inv, i_high, i_low, t_high, t_low)
    a2[z] = total(a1[rows_of(0, y * 32, 32)], sa, r_a2)
    sa = gather(a2.at[z], NZ, at_z)
    b2[z] = total(b1[rows_of(0, x * 32, 32)], sb, r_b2)
    sb = gather(b2.at[z], NZ, at_z)
    c1[...] = total(wst[rows_of(1024, z * 64, 64)], sc, r_c1)
    sc = scatter(lambda to: c1.at[rows_of(0, to * 16, 16)], 16, NX, at_x, x, r_c2)
    c2[y] = total(c1[rows_of(0, x * 16, 16)], sc, r_c2)
    sc = gather(c2.at[y], NY, at_y)
    arrived(sc)
    rows = rows_of(1024, z * 64 + x * 16, 16)
    wfull[k, rows] = c2[0] + c2[1] + c2[2] + c2[3]
    sc = gather(wfull.at[k, rows], NX, at_x)

    def over_z(ref):
        value = ref[0]
        for d in range(1, NZ):
            value = value + ref[d]
        return value

    arrived(sa)
    rows = rows_of(0, x * 128 + y * 32, 32)
    wfull[k, rows] = over_z(a2)
    sa = gather(wfull.at[k, rows], NY, at_y)
    arrived(sb)
    rows = rows_of(512, y * 128 + x * 32, 32)
    wfull[k, rows] = over_z(b2)
    sb = gather(wfull.at[k, rows], NX, at_x)
    arrived(sc)
    sc = gather(wfull.at[k, rows_of(1024, z * 64, 64)], NZ, at_z)
    arrived(sa)
    sa = gather(wfull.at[k, rows_of(0, x * 128, 128)], NX, at_x)
    arrived(sb)
    sb = gather(wfull.at[k, rows_of(512, y * 128, 128)], NY, at_y)
    finals = []
    for start, copies in ((0, sa), (512, sb), (1024, sc)):
        arrived(copies)
        third = wfull.at[k, pl.ds(start, 512)]
        finals.append(push(third, third, partner))
    out_rows[...] = dot6(p_rows[pl.ds(aligned(k, 64), 64)], inv[...])
    arrived(finals)
    finish_gradient(i_high, i_low, t_high, t_low, cmat, wfull, m_high, m_low, xmat, out_top)
    for copy in pending:
        copy.wait_send()


def odd(value, size):
    return value.reshape(HALF // (2 * size), 2, size, HALF)[:, 1].reshape(HALF // 2, HALF)


def inverse_pair(low, inv, which):
    rows, lanes = iota((HALF, HALF), 0), iota((HALF, HALF), 1)
    group = rows - lax.rem(rows, 8)
    within = iota((16, 8, HALF), 1)
    spans = [slice(which * BLOCK + HALF * i, which * BLOCK + HALF * i + HALF) for i in range(2)]
    owns = [low[span, span] for span in spans]
    values = [jnp.where(rows == lanes, 1.0, 0.0).reshape(16, 8, HALF)] * 2
    for step in range(8):
        for i in range(2):
            value = values[i]
            column = jnp.sum(jnp.where(lanes == group + step, owns[i], 0.0), axis=1, keepdims=True)
            column = jnp.broadcast_to(column, (HALF, HALF)).reshape(16, 8, HALF)
            solved = value[:, step : step + 1] / column[:, step : step + 1]
            solved = jnp.broadcast_to(solved, (16, 8, HALF))
            values[i] = jnp.where(within == step, solved, jnp.where(within > step, value - column * solved, value))
    values = [value.reshape(HALF, HALF) for value in values]
    for size in (8, 16, 32, 64):
        upper, left = lax.div(rows, size), lax.div(lanes, size)
        mask = jnp.logical_and(left + 1 == upper, lax.rem(upper, 2) == 1)
        inner = [dot6(odd(jnp.where(mask, owns[i], 0.0), size), values[i]) for i in range(2)]
        shape = (HALF // (2 * size), 1, size, HALF)
        none = jnp.zeros(shape, F32)
        inner = [jnp.concatenate([none, value.reshape(shape)], axis=1).reshape(HALF, HALF) for value in inner]
        inner = [dot6(odd(values[i], size), inner[i]) for i in range(2)]
        inner = [jnp.concatenate([none, value.reshape(shape)], axis=1).reshape(HALF, HALF) for value in inner]
        values = [values[i] - inner[i] for i in range(2)]
    first, second = spans
    inv[first, first] = values[0]
    inv[second, second] = values[1]
    inv[second, first] = -dot6(values[1], dot6(low[second, first], values[0]))
    inv[first, second] = jnp.zeros((HALF, HALF), F32)


def inverse_blocks(low, inv):
    one, two, three = slice(0, BLOCK), slice(BLOCK, 2 * BLOCK), slice(2 * BLOCK, 3 * BLOCK)
    inv[two, one] = -dot6(inv[two, two], dot6(low[two, one], inv[one, one]))
    inv[three, two] = -dot6(inv[three, three], dot6(low[three, two], inv[two, two]))
    inv[three, one] = -dot6(
        inv[three, three], dot6(low[three, one], inv[one, one]) + dot6(low[three, two], inv[two, one])
    )
    inv[one, 256:768] = jnp.zeros((BLOCK, 512), F32)
    inv[two, 512:768] = jnp.zeros((BLOCK, BLOCK), F32)


def inverse_halves(inv, i_high, i_low, t_high, t_low):
    for i in range(3):
        for j in range(i, 3):
            rows, lanes = slice(BLOCK * i, BLOCK * i + BLOCK), slice(BLOCK * j, BLOCK * j + BLOCK)
            value = inv[lanes, rows]
            i_high[lanes, rows], i_low[lanes, rows] = split(value)
            t_high[rows, lanes], t_low[rows, lanes] = split(value.T)


def start_gradient(low, topv, cmat):
    rows, lanes = iota((BLOCK, BLOCK), 0), iota((BLOCK, BLOCK), 1)
    for i in range(3):
        block = slice(BLOCK * i, BLOCK * i + BLOCK)
        flipped = low[BLOCK * i :, block].T
        for j in range(3):
            other = slice(BLOCK * j, BLOCK * j + BLOCK)
            if j > i:
                cmat[block, other] = jnp.zeros((BLOCK, BLOCK), F32)
                continue
            value = dot3(flipped, topv[BLOCK * i :, other])
            if i == j:
                value = jnp.where(rows > lanes, value, jnp.where(rows == lanes, 0.5 * value, 0.0))
            cmat[block, other] = value


def finish_gradient(i_high, i_low, t_high, t_low, cmat, wfull, m_high, m_low, xmat, out_top):
    rows, lanes = iota((BLOCK, HALF), 0), iota((BLOCK, HALF), 1)
    for block in range(3):
        for side in range(2):
            start = OFFSETS[block]
            column = slice(BLOCK * block + HALF * side, BLOCK * block + HALF * side + HALF)
            value = wfull[side, start : start + BLOCK]
            place = lanes + HALF * side
            value = jnp.where(rows > place, value, jnp.where(rows == place, 0.5 * value, 0.0))
            cmat[BLOCK * block : BLOCK * block + BLOCK, column] -= value
            if block < 2:
                end = start + WIDTH - BLOCK * block
                cmat[BLOCK * block + BLOCK :, column] -= wfull[side, start + BLOCK : end]
    def three(left_high, left_low, right_high, right_low):
        dims = ((1,), (0,))
        return (
            contract(left_low, right_high, dims) + contract(left_high, right_low, dims) + contract(left_high, right_high, dims)
        )

    for j in range(3):
        other = slice(BLOCK * j, BLOCK * j + BLOCK)
        c_high, c_low = split(cmat[BLOCK * j :, other])
        for i in range(3):
            block, start = slice(BLOCK * i, BLOCK * i + BLOCK), BLOCK * max(i, j)
            skip = start - BLOCK * j
            value = three(t_high[block, start:], t_low[block, start:], c_high[skip:], c_low[skip:])
            m_high[block, other], m_low[block, other] = split(value)
    for j in range(3):
        block, start = slice(BLOCK * j, BLOCK * j + BLOCK), BLOCK * j
        xmat[:, block] = three(m_high[:, start:], m_low[:, start:], i_high[start:, block], i_low[start:, block])
    rows, lanes = iota((BLOCK, BLOCK), 0), iota((BLOCK, BLOCK), 1)
    for i in range(3):
        for j in range(3):
            block, other = slice(BLOCK * i, BLOCK * i + BLOCK), slice(BLOCK * j, BLOCK * j + BLOCK)
            if j > i:
                out_top[block, other] = jnp.zeros((BLOCK, BLOCK), F32)
                continue
            value = xmat[block, other] + xmat[other, block].T
            if i == j:
                value = jnp.where(rows > lanes, value, jnp.where(rows == lanes, 0.5 * value, 0.0))
            out_top[block, other] = value


def per_device(trail_grad, factor_rows, factor_top, rows_grad, top_grad):
    anywhere = pl.BlockSpec(memory_space=pl.ANY)
    inside = pl.BlockSpec(memory_space=pltpu.VMEM)
    square, half_square = pltpu.VMEM((WIDTH, WIDTH), F32), pltpu.VMEM((WIDTH, WIDTH), BF16)

    def vmem(*shape):
        return pltpu.VMEM(shape, F32)

    return pl.pallas_call(
        kernel,
        out_shape=(jax.ShapeDtypeStruct((64, WIDTH), F32), jax.ShapeDtypeStruct((WIDTH, WIDTH), F32)),
        in_specs=[anywhere] * 5,
        out_specs=(inside, inside),
        scratch_shapes=[
            vmem(1024, 1024), pltpu.VMEM((1024, 1024), BF16), pltpu.VMEM((1024, 1024), BF16),
            vmem(WIDTH, 1024), vmem(4, GROUP, 1024), vmem(4, SUB, 1024), vmem(4, 8, SUB, 128), vmem(4, 4, SUB, 128),
            vmem(4, 4, SUB, 128), square, square, square, *[half_square] * 4, square, half_square, half_square, square, vmem(128, WIDTH), vmem(WIDTH, 128),
            vmem(128, WIDTH), vmem(NZ, CHUNK, 128), vmem(WIDTH, 128), vmem(1536, 128), vmem(3, 128, 128), vmem(3, 32, 128), vmem(128, 128),
            vmem(8, 32, 128), vmem(3, 128, 128), vmem(3, 32, 128), vmem(128, 128), vmem(8, 32, 128), vmem(7, 64, 128),
            vmem(3, 16, 128), vmem(64, 128), vmem(4, 16, 128), vmem(2, 1536, 128), pltpu.SemaphoreType.DMA((8,)),
            pltpu.SemaphoreType.DMA((SEMAPHORES,)), pltpu.SemaphoreType.DMA((SEMAPHORES,)),
        ],
        compiler_params=pltpu.CompilerParams(collective_id=0, has_side_effects=True, vmem_limit_bytes=62 << 20),
    )(trail_grad, factor_rows.T, factor_top, rows_grad, top_grad)


def solution(mesh):
    placed = (P("row", "col"), P("col", "row"), P(), P(("row", "col"), None), P())
    return jax.shard_map(
        per_device,
        mesh=mesh,
        in_specs=placed,
        out_specs=(P(("row", "col"), None), P()),
        check_vma=False,
    )
```

```python
import jax
import jax.numpy as jnp
from jax import lax
from jax.experimental import pallas as pl
from jax.experimental.pallas import tpu as pltpu
from jax.sharding import PartitionSpec as P

MESH = pl.DeviceIdType.MESH
F32, BF16 = jnp.float32, jnp.bfloat16
HIGHEST = lax.Precision.HIGHEST
NX, NY, NZ = 4, 4, 8
BLOCK, HALF, WIDTH = 256, 128, 768
CHUNK, PIECE = 48, 24
GROUP, SUB = 192, 96
OFFSETS = (0, 768, 1280)
SEMAPHORES = 200


def contract(left, right, dims, precision=None):
    return lax.dot_general(left, right, (dims, ((), ())), precision=precision, preferred_element_type=F32)


def split(value):
    high = value.astype(BF16)
    return high, (value - high.astype(F32)).astype(BF16)


def dot3(left, right, dims=((1,), (0,))):
    left_high, left_low = split(left)
    right_high, right_low = split(right)
    return (
        contract(left_low, right_high, dims)
        + contract(left_high, right_low, dims)
        + contract(left_high, right_high, dims)
    )


def dot6(left, right):
    return contract(left, right, ((1,), (0,)), HIGHEST)


def iota(shape, dim):
    return lax.broadcasted_iota(jnp.int32, shape, dim)


def aligned(index, unit):
    return pl.multiple_of(index * unit, unit)


def kernel(trail, factor, lower, grad, top, out_rows, out_top, strail, s_high, s_low, f_all, zt, cx, zc, r_left, r_right, low, topv,
           inv, i_high, i_low, t_high, t_low, cmat, m_high, m_low, xmat, gbuf, p_hat, p_rows, planes, f_here, wst, r_a1, r_a2, a1, a2, r_b1, r_b2, b1, b2, r_c1, r_c2, c1, c2,
           wfull, local_sem, send_sem, recv_sem):
    row, col = lax.axis_index("row"), lax.axis_index("col")
    y, x = lax.div(row, NX), lax.rem(row, NX)
    z, k = lax.div(col, 2), lax.rem(col, 2)
    other = 1 - k

    def at_x(d):
        return (y * NX + lax.rem(x + d + NX, NX), col)

    def at_y(d):
        return (lax.rem(y + d + NY, NY) * NX + x, col)

    def at_z(d):
        return (row, lax.rem(z + d + NZ, NZ) * 2 + k)

    partner = (row, z * 2 + other)
    count = [0]
    pending = []

    def push(src, dst, device):
        slot = count[0]
        count[0] += 1
        copy = pltpu.make_async_remote_copy(
            src_ref=src, dst_ref=dst, send_sem=send_sem.at[slot], recv_sem=recv_sem.at[slot], device_id=device, device_id_type=MESH
        )
        copy.start()
        pending.append(copy)
        return copy

    local = [
        pltpu.make_async_copy(factor, f_all.at[pl.ds(aligned(row, CHUNK), CHUNK)], local_sem.at[0]),
        pltpu.make_async_copy(grad, gbuf.at[pl.ds(aligned(k, 64), 64)], local_sem.at[1]),
        pltpu.make_async_copy(trail, strail, local_sem.at[2]),
        pltpu.make_async_copy(lower, low, local_sem.at[3]),
        pltpu.make_async_copy(top, topv, local_sem.at[4]),
    ]
    for copy in local:
        copy.start()

    barrier = pltpu.get_barrier_semaphore()

    def greet(device):
        pl.semaphore_signal(barrier, inc=1, device_id=device, device_id_type=MESH)

    for d in range(1, NX * NY):
        greet((lax.rem(row + d, NX * NY), col))
    for d in range(1, NZ):
        greet(at_z(d))
    greet(partner)
    pl.semaphore_wait(barrier, NX * NY + NZ - 1)

    local[0].wait()
    local[1].wait()

    rings = {"x": at_x, "y": at_y}

    def piece(ring, item, shift):
        if ring == "x":
            owner_x, owner_y = lax.rem(x + shift + NX, NX), y if item == 0 else lax.rem(y + item - 1, NY)
            offset = 0 if item == 0 else PIECE
        else:
            owner_y, owner_x = lax.rem(y + shift + NY, NY), x if item == 0 else lax.rem(x + item - 1, NX)
            offset = PIECE if item == 0 else 0
        return pl.ds(pl.multiple_of((owner_y * NX + owner_x) * CHUNK + offset, 8), PIECE)

    full, halves = {}, {}

    def send(ring, item):
        rows = f_all.at[piece(ring, item, 0)]
        full[ring, item] = [push(rows, rows, rings[ring](1)), push(rows, rows, rings[ring](-1))]

    def forward(ring, item):
        from_left, from_right = full[ring, item]
        from_left.wait_recv()
        rows = f_all.at[piece(ring, item, -1), pl.ds(0, 512)]
        right = push(rows, rows, rings[ring](1))
        from_right.wait_recv()
        rows = f_all.at[piece(ring, item, 1), pl.ds(512, 512)]
        halves[ring, item] = [right, push(rows, rows, rings[ring](-1))]

    def settle(ring, item):
        for copy in halves[ring, item]:
            copy.wait_recv()

    send("x", 0), send("y", 0), send("x", 1), send("y", 1)
    own_half = pl.ds(aligned(k, 64), 64)
    grad_copy = push(gbuf.at[own_half], gbuf.at[own_half], partner)
    chunk = pl.ds(aligned(row, CHUNK), CHUNK)
    spread = []
    for d in range(1, NZ):
        lanes = pl.ds(aligned(lax.rem(z + d, NZ), 128), 128)
        spread.append(push(f_all.at[chunk, lanes], planes.at[z], at_z(d)))
    keep = pltpu.make_async_copy(f_all.at[chunk, pl.ds(aligned(z, 128), 128)], planes.at[z], local_sem.at[5])
    keep.start()
    owner = lax.rem(row, 2) == k
    landing = f_here.at[chunk]
    pair = lax.div(row, 2)
    exchange, first_move, first_stay = [], [], []

    def rearrange():
        keep.wait()
        for copy in spread:
            copy.wait_recv()
        for d in range(NZ):
            block = lax.rem(pair + d, NZ)
            copy = pltpu.make_async_remote_copy(
                src_ref=planes.at[block], dst_ref=landing, send_sem=send_sem.at[SEMAPHORES - 2 - d],
                recv_sem=recv_sem.at[SEMAPHORES - 1], device_id=(block * 2 + k, col), device_id_type=MESH,
            )
            if d == 0:
                first_move.append(copy)
                first_stay.append(pltpu.make_async_copy(planes.at[block], landing, local_sem.at[6]))
            else:
                copy.start()
                exchange.append(copy)

        @pl.when(jnp.logical_not(owner))
        def _():
            first_move[0].start()

        @pl.when(owner)
        def _():
            first_stay[0].start()

    share = pltpu.make_async_remote_copy(
        src_ref=f_here, dst_ref=f_here, send_sem=send_sem.at[SEMAPHORES - 10], recv_sem=recv_sem.at[SEMAPHORES - 10],
        device_id=partner, device_id_type=MESH,
    )

    def pass_on():
        for copy in exchange:
            copy.wait_send()

        @pl.when(owner)
        def _():
            most = f_here.at[0 : WIDTH - CHUNK]
            pltpu.make_async_remote_copy(
                src_ref=most, dst_ref=most, send_sem=send_sem.at[SEMAPHORES - 1], recv_sem=recv_sem.at[SEMAPHORES - 1],
                device_id=partner, device_id_type=MESH,
            ).wait_recv()
            first_stay[0].wait()
            share.start()

        @pl.when(jnp.logical_not(owner))
        def _():
            first_move[0].wait_send()

    def passed():
        @pl.when(owner)
        def _():
            share.wait_send()

        @pl.when(jnp.logical_not(owner))
        def _():
            share.wait_recv()

    local[2].wait()

    @pl.loop(0, 8)
    def _(step):
        rows = pl.ds(aligned(step, 128), 128)
        s_high[rows], s_low[rows] = split(strail[rows])

    forward("x", 0), forward("y", 0)
    send("x", 2), send("y", 2)
    forward("x", 1), forward("y", 1)
    send("x", 4), send("y", 4)
    settle("x", 0), settle("y", 0)
    send("x", 3), send("y", 3)
    grad_copy.wait_recv()
    cmat[:, 0:128] = gbuf[...].T
    for j in range(4):
        rows = pl.ds(pl.multiple_of(j * GROUP + k * SUB, 8), SUB)
        p_hat[rows] = cmat[rows, 0:128]
    settle("x", 1)

    def multiply(*groups):
        parts = [split(f_all[pl.ds(aligned(lax.rem(y + j, NY), GROUP), GROUP)]) for j in groups]
        high = jnp.concatenate([part[0] for part in parts], axis=0)
        both = jnp.concatenate([part[0] for part in parts] + [part[1] for part in parts], axis=0)
        size = GROUP * len(groups)

        @pl.loop(0, 4)
        def _(step):
            part = pl.ds(aligned(step, BLOCK), BLOCK)
            dims = ((1,), (1,))
            first = contract(both, s_high[part], dims)
            value = first[:size] + first[size:] + contract(high, s_low[part], dims)
            for i, j in enumerate(groups):
                zt[j, :, part] = value[GROUP * i : GROUP * i + GROUP]

    crossing = {}

    def cross(j):
        crossing[j] = push(zt.at[j, pl.ds(aligned(other, SUB), SUB)], cx.at[j], partner)

    lefts, rights = {}, {}

    def begin(j):
        crossing[j].wait_recv()
        own = pl.ds(aligned(k, SUB), SUB)
        for d in range(NZ):
            lanes = pl.ds(128 * d, 128)
            zc[j, d] = zt[j, own, lanes] + cx[j, :, lanes]
        far = lax.rem(z + 4, NZ)
        lefts[j] = push(zc.at[j, far, pl.ds(0, 48)], r_left.at[j, 0, pl.ds(0, 48)], at_z(-1))
        rights[j] = push(zc.at[j, far, pl.ds(48, 48)], r_right.at[j, 0, pl.ds(48, 48)], at_z(1))

    def travel(j, step):
        to_left, to_right = lax.rem(z + 3 + step, NZ), lax.rem(z + 5 - step, NZ)
        lefts[j].wait_recv()
        if step == 2:
            zc[j, to_left, 0:48] += r_left[j, 0, 0:48]
        else:
            zc[j, to_left] += r_left[j, step - 2]
        lefts[j] = push(zc.at[j, to_left], r_left.at[j, step - 1], at_z(-1))
        rights[j].wait_recv()
        if step == 2:
            zc[j, to_right, 48:96] += r_right[j, 0, 48:96]
        else:
            zc[j, to_right] += r_right[j, step - 2]
        rights[j] = push(zc.at[j, to_right], r_right.at[j, step - 1], at_z(1))

    shares = []

    def arrive(j):
        lefts[j].wait_recv()
        rights[j].wait_recv()
        rows = pl.ds(pl.multiple_of(lax.rem(y + j, NY) * GROUP + k * SUB, 8), SUB)
        p_hat[rows] = p_hat[rows] - 2.0 * (zc[j, z] + r_left[j, 3] + r_right[j, 3])
        shares.append(push(p_hat.at[rows], p_hat.at[rows], partner))

    multiply(0)
    cross(0)
    forward("x", 2), forward("y", 2), forward("x", 4), forward("y", 4)
    begin(0)
    forward("x", 3), forward("y", 3)
    rearrange()
    travel(0, 2)
    settle("x", 2), settle("x", 4)
    multiply(1, 3)
    cross(1)
    cross(3)
    travel(0, 3)
    for ring, item in (("y", 1), ("y", 2), ("y", 3), ("y", 4), ("x", 3)):
        settle(ring, item)
    multiply(2)
    cross(2)
    travel(0, 4)
    begin(1)
    begin(3)
    pass_on()
    begin(2)
    travel(1, 2)
    travel(3, 2)
    arrive(0)
    travel(2, 2)
    local[3].wait()
    inverse_pair(low, inv, 0)
    travel(1, 3)
    travel(3, 3)
    travel(2, 3)
    travel(1, 4)
    travel(3, 4)
    travel(2, 4)
    arrive(1)
    arrive(3)
    arrive(2)
    for copy in shares:
        copy.wait_recv()
    passed()

    for block in range(3):
        start = OFFSETS[block]
        rows = WIDTH - BLOCK * block
        wst[start : start + rows] = dot3(p_hat[BLOCK * block :], f_here[pl.ds(pl.multiple_of(block * BLOCK + k * HALF, HALF), HALF)], ((1,), (1,)))

    def scatter(src, unit, extent, reach, me, buffer):
        copies = []
        for d in range(1, extent):
            to = lax.rem(me + d, extent)
            copies.append(push(src(to), buffer.at[d - 1], reach(d)))
        return copies

    def total(own, copies, buffer):
        for d, copy in enumerate(copies):
            copy.wait_recv()
            own = own + buffer[d]
        return own

    def gather(ref, extent, reach):
        return [push(ref, ref, reach(d)) for d in range(1, extent)]

    def arrived(copies):
        for copy in copies:
            copy.wait_recv()

    def rows_of(base, start, size):
        return pl.ds(pl.multiple_of(base + start, 8), size)

    sc = scatter(lambda to: wst.at[rows_of(1024, to * 64, 64)], 64, NZ, at_z, z, r_c1)
    sa = scatter(lambda to: wst.at[rows_of(0, to * 128, 128)], 128, NX, at_x, x, r_a1)
    sb = scatter(lambda to: wst.at[rows_of(512, to * 128, 128)], 128, NY, at_y, y, r_b1)
    p_rows[...] = p_hat[...].T
    inverse_pair(low, inv, 1)
    a1[...] = total(wst[rows_of(0, x * 128, 128)], sa, r_a1)
    sa = scatter(lambda to: a1.at[rows_of(0, to * 32, 32)], 32, NY, at_y, y, r_a2)
    b1[...] = total(wst[rows_of(512, y * 128, 128)], sb, r_b1)
    sb = scatter(lambda to: b1.at[rows_of(0, to * 32, 32)], 32, NX, at_x, x, r_b2)
    inverse_pair(low, inv, 2)
    a2[z] = total(a1[rows_of(0, y * 32, 32)], sa, r_a2)
    sa = gather(a2.at[z], NZ, at_z)
    b2[z] = total(b1[rows_of(0, x * 32, 32)], sb, r_b2)
    sb = gather(b2.at[z], NZ, at_z)
    c1[...] = total(wst[rows_of(1024, z * 64, 64)], sc, r_c1)
    sc = scatter(lambda to: c1.at[rows_of(0, to * 16, 16)], 16, NX, at_x, x, r_c2)
    inverse_blocks(low, inv)
    c2[y] = total(c1[rows_of(0, x * 16, 16)], sc, r_c2)
    sc = gather(c2.at[y], NY, at_y)
    inverse_halves(inv, i_high, i_low, t_high, t_low)
    local[4].wait()
    start_gradient(low, topv, cmat)
    arrived(sc)
    rows = rows_of(1024, z * 64 + x * 16, 16)
    wfull[k, rows] = c2[0] + c2[1] + c2[2] + c2[3]
    sc = gather(wfull.at[k, rows], NX, at_x)
    out_rows[...] = dot6(p_rows[pl.ds(aligned(k, 64), 64)], inv[...])

    def over_z(ref):
        value = ref[0]
        for d in range(1, NZ):
            value = value + ref[d]
        return value

    arrived(sa)
    rows = rows_of(0, x * 128 + y * 32, 32)
    wfull[k, rows] = over_z(a2)
    sa = gather(wfull.at[k, rows], NY, at_y)
    arrived(sb)
    rows = rows_of(512, y * 128 + x * 32, 32)
    wfull[k, rows] = over_z(b2)
    sb = gather(wfull.at[k, rows], NX, at_x)
    arrived(sc)
    sc = gather(wfull.at[k, rows_of(1024, z * 64, 64)], NZ, at_z)
    arrived(sa)
    sa = gather(wfull.at[k, rows_of(0, x * 128, 128)], NX, at_x)
    arrived(sb)
    sb = gather(wfull.at[k, rows_of(512, y * 128, 128)], NY, at_y)
    finals = []

    def hand_over(base, size, extent, me, copies):
        def give(owner):
            block = wfull.at[k, rows_of(base, owner * size, size)]
            finals.append(push(block, block, partner))

        give(me)
        order = sorted(range(1, extent), key=lambda d: min(d, extent - d))
        for d in order:
            copies[d - 1].wait_recv()
            give(lax.rem(me - d + extent, extent))

    hand_over(0, 128, NX, x, sa)
    hand_over(512, 128, NY, y, sb)
    hand_over(1024, 64, NZ, z, sc)
    arrived(finals)
    finish_gradient(i_high, i_low, t_high, t_low, cmat, wfull, m_high, m_low, xmat, out_top)
    for copy in pending:
        copy.wait_send()


def odd(value, size):
    return value.reshape(HALF // (2 * size), 2, size, HALF)[:, 1].reshape(HALF // 2, HALF)


def inverse_pair(low, inv, which):
    rows, lanes = iota((HALF, HALF), 0), iota((HALF, HALF), 1)
    group = rows - lax.rem(rows, 8)
    within = iota((16, 8, HALF), 1)
    spans = [slice(which * BLOCK + HALF * i, which * BLOCK + HALF * i + HALF) for i in range(2)]
    owns = [low[span, span] for span in spans]
    values = [jnp.where(rows == lanes, 1.0, 0.0).reshape(16, 8, HALF)] * 2
    for step in range(8):
        for i in range(2):
            value = values[i]
            column = jnp.sum(jnp.where(lanes == group + step, owns[i], 0.0), axis=1, keepdims=True)
            column = jnp.broadcast_to(column, (HALF, HALF)).reshape(16, 8, HALF)
            solved = value[:, step : step + 1] / column[:, step : step + 1]
            solved = jnp.broadcast_to(solved, (16, 8, HALF))
            values[i] = jnp.where(within == step, solved, jnp.where(within > step, value - column * solved, value))
    values = [value.reshape(HALF, HALF) for value in values]
    for size in (8, 16, 32, 64):
        upper, left = lax.div(rows, size), lax.div(lanes, size)
        mask = jnp.logical_and(left + 1 == upper, lax.rem(upper, 2) == 1)
        inner = [dot6(odd(jnp.where(mask, owns[i], 0.0), size), values[i]) for i in range(2)]
        shape = (HALF // (2 * size), 1, size, HALF)
        none = jnp.zeros(shape, F32)
        inner = [jnp.concatenate([none, value.reshape(shape)], axis=1).reshape(HALF, HALF) for value in inner]
        inner = [dot6(odd(values[i], size), inner[i]) for i in range(2)]
        inner = [jnp.concatenate([none, value.reshape(shape)], axis=1).reshape(HALF, HALF) for value in inner]
        values = [values[i] - inner[i] for i in range(2)]
    first, second = spans
    inv[first, first] = values[0]
    inv[second, second] = values[1]
    inv[second, first] = -dot6(values[1], dot6(low[second, first], values[0]))
    inv[first, second] = jnp.zeros((HALF, HALF), F32)


def inverse_blocks(low, inv):
    one, two, three = slice(0, BLOCK), slice(BLOCK, 2 * BLOCK), slice(2 * BLOCK, 3 * BLOCK)
    inv[two, one] = -dot6(inv[two, two], dot6(low[two, one], inv[one, one]))
    inv[three, two] = -dot6(inv[three, three], dot6(low[three, two], inv[two, two]))
    inv[three, one] = -dot6(
        inv[three, three], dot6(low[three, one], inv[one, one]) + dot6(low[three, two], inv[two, one])
    )
    inv[one, 256:768] = jnp.zeros((BLOCK, 512), F32)
    inv[two, 512:768] = jnp.zeros((BLOCK, BLOCK), F32)


def inverse_halves(inv, i_high, i_low, t_high, t_low):
    for i in range(3):
        for j in range(i, 3):
            rows, lanes = slice(BLOCK * i, BLOCK * i + BLOCK), slice(BLOCK * j, BLOCK * j + BLOCK)
            value = inv[lanes, rows]
            i_high[lanes, rows], i_low[lanes, rows] = split(value)
            t_high[rows, lanes], t_low[rows, lanes] = split(value.T)


def start_gradient(low, topv, cmat):
    rows, lanes = iota((BLOCK, BLOCK), 0), iota((BLOCK, BLOCK), 1)
    for i in range(3):
        block = slice(BLOCK * i, BLOCK * i + BLOCK)
        flipped = low[BLOCK * i :, block].T
        for j in range(3):
            other = slice(BLOCK * j, BLOCK * j + BLOCK)
            if j > i:
                cmat[block, other] = jnp.zeros((BLOCK, BLOCK), F32)
                continue
            value = dot3(flipped, topv[BLOCK * i :, other])
            if i == j:
                value = jnp.where(rows > lanes, value, jnp.where(rows == lanes, 0.5 * value, 0.0))
            cmat[block, other] = value


def finish_gradient(i_high, i_low, t_high, t_low, cmat, wfull, m_high, m_low, xmat, out_top):
    rows, lanes = iota((BLOCK, HALF), 0), iota((BLOCK, HALF), 1)
    for block in range(3):
        for side in range(2):
            start = OFFSETS[block]
            column = slice(BLOCK * block + HALF * side, BLOCK * block + HALF * side + HALF)
            value = wfull[side, start : start + BLOCK]
            place = lanes + HALF * side
            value = jnp.where(rows > place, value, jnp.where(rows == place, 0.5 * value, 0.0))
            cmat[BLOCK * block : BLOCK * block + BLOCK, column] -= value
            if block < 2:
                end = start + WIDTH - BLOCK * block
                cmat[BLOCK * block + BLOCK :, column] -= wfull[side, start + BLOCK : end]
    def three(left_high, left_low, right_high, right_low):
        dims = ((1,), (0,))
        return (
            contract(left_low, right_high, dims) + contract(left_high, right_low, dims) + contract(left_high, right_high, dims)
        )

    for j in range(3):
        other = slice(BLOCK * j, BLOCK * j + BLOCK)
        c_high, c_low = split(cmat[BLOCK * j :, other])
        for i in range(3):
            block, start = slice(BLOCK * i, BLOCK * i + BLOCK), BLOCK * max(i, j)
            skip = start - BLOCK * j
            value = three(t_high[block, start:], t_low[block, start:], c_high[skip:], c_low[skip:])
            m_high[block, other], m_low[block, other] = split(value)
    for j in range(3):
        block, start = slice(BLOCK * j, BLOCK * j + BLOCK), BLOCK * j
        xmat[:, block] = three(m_high[:, start:], m_low[:, start:], i_high[start:, block], i_low[start:, block])
    rows, lanes = iota((BLOCK, BLOCK), 0), iota((BLOCK, BLOCK), 1)
    for i in range(3):
        for j in range(3):
            block, other = slice(BLOCK * i, BLOCK * i + BLOCK), slice(BLOCK * j, BLOCK * j + BLOCK)
            if j > i:
                out_top[block, other] = jnp.zeros((BLOCK, BLOCK), F32)
                continue
            value = xmat[block, other] + xmat[other, block].T
            if i == j:
                value = jnp.where(rows > lanes, value, jnp.where(rows == lanes, 0.5 * value, 0.0))
            out_top[block, other] = value


def per_device(trail_grad, factor_rows, factor_top, rows_grad, top_grad):
    anywhere = pl.BlockSpec(memory_space=pl.ANY)
    inside = pl.BlockSpec(memory_space=pltpu.VMEM)
    square, half_square = pltpu.VMEM((WIDTH, WIDTH), F32), pltpu.VMEM((WIDTH, WIDTH), BF16)

    def vmem(*shape):
        return pltpu.VMEM(shape, F32)

    return pl.pallas_call(
        kernel,
        out_shape=(jax.ShapeDtypeStruct((64, WIDTH), F32), jax.ShapeDtypeStruct((WIDTH, WIDTH), F32)),
        in_specs=[anywhere] * 5,
        out_specs=(inside, inside),
        scratch_shapes=[
            vmem(1024, 1024), pltpu.VMEM((1024, 1024), BF16), pltpu.VMEM((1024, 1024), BF16),
            vmem(WIDTH, 1024), vmem(4, GROUP, 1024), vmem(4, SUB, 1024), vmem(4, 8, SUB, 128), vmem(4, 4, SUB, 128),
            vmem(4, 4, SUB, 128), square, square, square, *[half_square] * 4, square, half_square, half_square, square, vmem(128, WIDTH), vmem(WIDTH, 128),
            vmem(128, WIDTH), vmem(NZ, CHUNK, 128), vmem(WIDTH, 128), vmem(1536, 128), vmem(3, 128, 128), vmem(3, 32, 128), vmem(128, 128),
            vmem(8, 32, 128), vmem(3, 128, 128), vmem(3, 32, 128), vmem(128, 128), vmem(8, 32, 128), vmem(7, 64, 128),
            vmem(3, 16, 128), vmem(64, 128), vmem(4, 16, 128), vmem(2, 1536, 128), pltpu.SemaphoreType.DMA((8,)),
            pltpu.SemaphoreType.DMA((SEMAPHORES,)), pltpu.SemaphoreType.DMA((SEMAPHORES,)),
        ],
        compiler_params=pltpu.CompilerParams(collective_id=0, has_side_effects=True, vmem_limit_bytes=62 << 20),
    )(trail_grad, factor_rows.T, factor_top, rows_grad, top_grad)


def solution(mesh):
    placed = (P("row", "col"), P("col", "row"), P(), P(("row", "col"), None), P())
    return jax.shard_map(
        per_device,
        mesh=mesh,
        in_specs=placed,
        out_specs=(P(("row", "col"), None), P()),
        check_vma=False,
    )
```

```python
import jax
import jax.numpy as jnp
from jax import lax
from jax.experimental import pallas as pl
from jax.experimental.pallas import tpu as pltpu
from jax.sharding import PartitionSpec as P

MESH = pl.DeviceIdType.MESH
F32, BF16 = jnp.float32, jnp.bfloat16
HIGHEST = lax.Precision.HIGHEST
NX, NY, NZ = 4, 4, 8
BLOCK, HALF, WIDTH = 256, 128, 768
CHUNK, PIECE = 48, 24
GROUP, SUB = 192, 96
OFFSETS = (0, 768, 1280)
SEMAPHORES = 200


def contract(left, right, dims, precision=None):
    return lax.dot_general(left, right, (dims, ((), ())), precision=precision, preferred_element_type=F32)


def split(value):
    high = value.astype(BF16)
    return high, (value - high.astype(F32)).astype(BF16)


def dot3(left, right, dims=((1,), (0,))):
    left_high, left_low = split(left)
    right_high, right_low = split(right)
    return (
        contract(left_low, right_high, dims)
        + contract(left_high, right_low, dims)
        + contract(left_high, right_high, dims)
    )


def dot6(left, right):
    return contract(left, right, ((1,), (0,)), HIGHEST)


def iota(shape, dim):
    return lax.broadcasted_iota(jnp.int32, shape, dim)


def aligned(index, unit):
    return pl.multiple_of(index * unit, unit)


def kernel(trail, factor, lower, grad, top, out_rows, out_top, strail, s_high, s_low, f_all, zt, cx, zc, r_left, r_right, low, topv,
           inv, i_high, i_low, t_high, t_low, cmat, m_high, m_low, xmat, gbuf, p_hat, p_rows, planes, f_here, wst, r_a1, r_a2, a1, a2, r_b1, r_b2, b1, b2, r_c1, r_c2, c1, c2,
           wfull, rows_v, top_v, local_sem, send_sem, recv_sem):
    row, col = lax.axis_index("row"), lax.axis_index("col")
    y, x = lax.div(row, NX), lax.rem(row, NX)
    z, k = lax.div(col, 2), lax.rem(col, 2)
    other = 1 - k

    def at_x(d):
        return (y * NX + lax.rem(x + d + NX, NX), col)

    def at_y(d):
        return (lax.rem(y + d + NY, NY) * NX + x, col)

    def at_z(d):
        return (row, lax.rem(z + d + NZ, NZ) * 2 + k)

    partner = (row, z * 2 + other)
    count = [0]
    pending = []

    def push(src, dst, device):
        slot = count[0]
        count[0] += 1
        copy = pltpu.make_async_remote_copy(
            src_ref=src, dst_ref=dst, send_sem=send_sem.at[slot], recv_sem=recv_sem.at[slot], device_id=device, device_id_type=MESH
        )
        copy.start()
        pending.append(copy)
        return copy

    local = [
        pltpu.make_async_copy(factor, f_all.at[pl.ds(aligned(row, CHUNK), CHUNK)], local_sem.at[0]),
        pltpu.make_async_copy(grad, gbuf.at[pl.ds(aligned(k, 64), 64)], local_sem.at[1]),
        pltpu.make_async_copy(trail, strail, local_sem.at[2]),
        pltpu.make_async_copy(lower, low, local_sem.at[3]),
        pltpu.make_async_copy(top, topv, local_sem.at[4]),
    ]
    for copy in local:
        copy.start()

    barrier = pltpu.get_barrier_semaphore()

    def greet(device):
        pl.semaphore_signal(barrier, inc=1, device_id=device, device_id_type=MESH)

    for d in range(1, NX * NY):
        greet((lax.rem(row + d, NX * NY), col))
    for d in range(1, NZ):
        greet(at_z(d))
    greet(partner)
    pl.semaphore_wait(barrier, NX * NY + NZ - 1)

    local[0].wait()
    local[1].wait()

    rings = {"x": at_x, "y": at_y}

    def piece(ring, item, shift):
        if ring == "x":
            owner_x, owner_y = lax.rem(x + shift + NX, NX), y if item == 0 else lax.rem(y + item - 1, NY)
            offset = 0 if item == 0 else PIECE
        else:
            owner_y, owner_x = lax.rem(y + shift + NY, NY), x if item == 0 else lax.rem(x + item - 1, NX)
            offset = PIECE if item == 0 else 0
        return pl.ds(pl.multiple_of((owner_y * NX + owner_x) * CHUNK + offset, 8), PIECE)

    full, halves = {}, {}

    def send(ring, item):
        rows = f_all.at[piece(ring, item, 0)]
        full[ring, item] = [push(rows, rows, rings[ring](1)), push(rows, rows, rings[ring](-1))]

    def forward(ring, item):
        from_left, from_right = full[ring, item]
        from_left.wait_recv()
        rows = f_all.at[piece(ring, item, -1), pl.ds(0, 512)]
        right = push(rows, rows, rings[ring](1))
        from_right.wait_recv()
        rows = f_all.at[piece(ring, item, 1), pl.ds(512, 512)]
        halves[ring, item] = [right, push(rows, rows, rings[ring](-1))]

    def settle(ring, item):
        for copy in halves[ring, item]:
            copy.wait_recv()

    send("x", 0), send("y", 0), send("x", 1), send("y", 1)
    own_half = pl.ds(aligned(k, 64), 64)
    grad_copy = push(gbuf.at[own_half], gbuf.at[own_half], partner)
    chunk = pl.ds(aligned(row, CHUNK), CHUNK)
    spread = []
    for d in range(1, NZ):
        lanes = pl.ds(aligned(lax.rem(z + d, NZ), 128), 128)
        spread.append(push(f_all.at[chunk, lanes], planes.at[z], at_z(d)))
    keep = pltpu.make_async_copy(f_all.at[chunk, pl.ds(aligned(z, 128), 128)], planes.at[z], local_sem.at[5])
    keep.start()
    owner = lax.rem(row, 2) == k
    landing = f_here.at[chunk]
    pair = lax.div(row, 2)
    exchange, first_move, first_stay = [], [], []

    def rearrange():
        keep.wait()
        for copy in spread:
            copy.wait_recv()
        for d in range(NZ):
            block = lax.rem(pair + d, NZ)
            copy = pltpu.make_async_remote_copy(
                src_ref=planes.at[block], dst_ref=landing, send_sem=send_sem.at[SEMAPHORES - 2 - d],
                recv_sem=recv_sem.at[SEMAPHORES - 1], device_id=(block * 2 + k, col), device_id_type=MESH,
            )
            if d == 0:
                first_move.append(copy)
                first_stay.append(pltpu.make_async_copy(planes.at[block], landing, local_sem.at[6]))
            else:
                copy.start()
                exchange.append(copy)

        @pl.when(jnp.logical_not(owner))
        def _():
            first_move[0].start()

        @pl.when(owner)
        def _():
            first_stay[0].start()

    share = pltpu.make_async_remote_copy(
        src_ref=f_here, dst_ref=f_here, send_sem=send_sem.at[SEMAPHORES - 10], recv_sem=recv_sem.at[SEMAPHORES - 10],
        device_id=partner, device_id_type=MESH,
    )

    def pass_on():
        for copy in exchange:
            copy.wait_send()

        @pl.when(owner)
        def _():
            most = f_here.at[0 : WIDTH - CHUNK]
            pltpu.make_async_remote_copy(
                src_ref=most, dst_ref=most, send_sem=send_sem.at[SEMAPHORES - 1], recv_sem=recv_sem.at[SEMAPHORES - 1],
                device_id=partner, device_id_type=MESH,
            ).wait_recv()
            first_stay[0].wait()
            share.start()

        @pl.when(jnp.logical_not(owner))
        def _():
            first_move[0].wait_send()

    def passed():
        @pl.when(owner)
        def _():
            share.wait_send()

        @pl.when(jnp.logical_not(owner))
        def _():
            share.wait_recv()

    local[2].wait()

    @pl.loop(0, 8)
    def _(step):
        rows = pl.ds(aligned(step, 128), 128)
        s_high[rows], s_low[rows] = split(strail[rows])

    forward("x", 0), forward("y", 0)
    send("x", 2), send("y", 2)
    forward("x", 1), forward("y", 1)
    send("x", 4), send("y", 4)
    settle("x", 0), settle("y", 0)
    send("x", 3), send("y", 3)
    grad_copy.wait_recv()
    cmat[:, 0:128] = gbuf[...].T
    for j in range(4):
        rows = pl.ds(pl.multiple_of(j * GROUP + k * SUB, 8), SUB)
        p_hat[rows] = cmat[rows, 0:128]
    settle("x", 1)

    def multiply(*groups):
        parts = [split(f_all[pl.ds(aligned(lax.rem(y + j, NY), GROUP), GROUP)]) for j in groups]
        high = jnp.concatenate([part[0] for part in parts], axis=0)
        both = jnp.concatenate([part[0] for part in parts] + [part[1] for part in parts], axis=0)
        size = GROUP * len(groups)

        @pl.loop(0, 4)
        def _(step):
            part = pl.ds(aligned(step, BLOCK), BLOCK)
            dims = ((1,), (1,))
            first = contract(both, s_high[part], dims)
            value = first[:size] + first[size:] + contract(high, s_low[part], dims)
            for i, j in enumerate(groups):
                zt[j, :, part] = value[GROUP * i : GROUP * i + GROUP]

    crossing = {}

    def cross(j):
        crossing[j] = push(zt.at[j, pl.ds(aligned(other, SUB), SUB)], cx.at[j], partner)

    lefts, rights = {}, {}

    def begin(j):
        crossing[j].wait_recv()
        own = pl.ds(aligned(k, SUB), SUB)
        for d in range(NZ):
            lanes = pl.ds(128 * d, 128)
            zc[j, d] = zt[j, own, lanes] + cx[j, :, lanes]
        far = lax.rem(z + 4, NZ)
        lefts[j] = push(zc.at[j, far, pl.ds(0, 48)], r_left.at[j, 0, pl.ds(0, 48)], at_z(-1))
        rights[j] = push(zc.at[j, far, pl.ds(48, 48)], r_right.at[j, 0, pl.ds(48, 48)], at_z(1))

    def travel(j, step):
        to_left, to_right = lax.rem(z + 3 + step, NZ), lax.rem(z + 5 - step, NZ)
        lefts[j].wait_recv()
        if step == 2:
            zc[j, to_left, 0:48] += r_left[j, 0, 0:48]
        else:
            zc[j, to_left] += r_left[j, step - 2]
        lefts[j] = push(zc.at[j, to_left], r_left.at[j, step - 1], at_z(-1))
        rights[j].wait_recv()
        if step == 2:
            zc[j, to_right, 48:96] += r_right[j, 0, 48:96]
        else:
            zc[j, to_right] += r_right[j, step - 2]
        rights[j] = push(zc.at[j, to_right], r_right.at[j, step - 1], at_z(1))

    shares = []

    def arrive(j):
        lefts[j].wait_recv()
        rights[j].wait_recv()
        rows = pl.ds(pl.multiple_of(lax.rem(y + j, NY) * GROUP + k * SUB, 8), SUB)
        p_hat[rows] = p_hat[rows] - 2.0 * (zc[j, z] + r_left[j, 3] + r_right[j, 3])
        shares.append(push(p_hat.at[rows], p_hat.at[rows], partner))

    multiply(0)
    cross(0)
    forward("x", 2), forward("y", 2), forward("x", 4), forward("y", 4)
    begin(0)
    forward("x", 3), forward("y", 3)
    rearrange()
    travel(0, 2)
    settle("x", 2), settle("x", 4)
    multiply(1, 3)
    cross(1)
    cross(3)
    travel(0, 3)
    for ring, item in (("y", 1), ("y", 2), ("y", 3), ("y", 4), ("x", 3)):
        settle(ring, item)
    multiply(2)
    cross(2)
    travel(0, 4)
    begin(1)
    begin(3)
    pass_on()
    begin(2)
    travel(1, 2)
    travel(3, 2)
    arrive(0)
    travel(2, 2)
    local[3].wait()
    inverse_pair(low, inv, 0)
    travel(1, 3)
    travel(3, 3)
    travel(2, 3)
    travel(1, 4)
    travel(3, 4)
    travel(2, 4)
    arrive(1)
    arrive(3)
    arrive(2)
    for copy in shares:
        copy.wait_recv()
    passed()

    for block in range(3):
        start = OFFSETS[block]
        rows = WIDTH - BLOCK * block
        wst[start : start + rows] = dot3(p_hat[BLOCK * block :], f_here[pl.ds(pl.multiple_of(block * BLOCK + k * HALF, HALF), HALF)], ((1,), (1,)))

    def scatter(src, unit, extent, reach, me, buffer):
        copies = []
        for d in range(1, extent):
            to = lax.rem(me + d, extent)
            copies.append(push(src(to), buffer.at[d - 1], reach(d)))
        return copies

    def total(own, copies, buffer):
        for d, copy in enumerate(copies):
            copy.wait_recv()
            own = own + buffer[d]
        return own

    def gather(ref, extent, reach):
        return [push(ref, ref, reach(d)) for d in range(1, extent)]

    def arrived(copies):
        for copy in copies:
            copy.wait_recv()

    def rows_of(base, start, size):
        return pl.ds(pl.multiple_of(base + start, 8), size)

    sc = scatter(lambda to: wst.at[rows_of(1024, to * 64, 64)], 64, NZ, at_z, z, r_c1)
    sa = scatter(lambda to: wst.at[rows_of(0, to * 128, 128)], 128, NX, at_x, x, r_a1)
    sb = scatter(lambda to: wst.at[rows_of(512, to * 128, 128)], 128, NY, at_y, y, r_b1)
    p_rows[...] = p_hat[...].T
    inverse_pair(low, inv, 1)
    a1[...] = total(wst[rows_of(0, x * 128, 128)], sa, r_a1)
    sa = scatter(lambda to: a1.at[rows_of(0, to * 32, 32)], 32, NY, at_y, y, r_a2)
    b1[...] = total(wst[rows_of(512, y * 128, 128)], sb, r_b1)
    sb = scatter(lambda to: b1.at[rows_of(0, to * 32, 32)], 32, NX, at_x, x, r_b2)
    inverse_pair(low, inv, 2)
    a2[z] = total(a1[rows_of(0, y * 32, 32)], sa, r_a2)
    sa = gather(a2.at[z], NZ, at_z)
    b2[z] = total(b1[rows_of(0, x * 32, 32)], sb, r_b2)
    sb = gather(b2.at[z], NZ, at_z)
    c1[...] = total(wst[rows_of(1024, z * 64, 64)], sc, r_c1)
    sc = scatter(lambda to: c1.at[rows_of(0, to * 16, 16)], 16, NX, at_x, x, r_c2)
    inverse_blocks(low, inv)
    c2[y] = total(c1[rows_of(0, x * 16, 16)], sc, r_c2)
    sc = gather(c2.at[y], NY, at_y)
    inverse_halves(inv, i_high, i_low, t_high, t_low)
    local[4].wait()
    start_gradient(low, topv, cmat)
    arrived(sc)
    rows = rows_of(1024, z * 64 + x * 16, 16)
    wfull[k, rows] = c2[0] + c2[1] + c2[2] + c2[3]
    sc = gather(wfull.at[k, rows], NX, at_x)
    rows_v[...] = dot6(p_rows[pl.ds(aligned(k, 64), 64)], inv[...])
    written = [pltpu.make_async_copy(rows_v, out_rows, local_sem.at[7])]
    written[0].start()

    def over_z(ref):
        value = ref[0]
        for d in range(1, NZ):
            value = value + ref[d]
        return value

    arrived(sa)
    rows = rows_of(0, x * 128 + y * 32, 32)
    wfull[k, rows] = over_z(a2)
    sa = gather(wfull.at[k, rows], NY, at_y)
    arrived(sb)
    rows = rows_of(512, y * 128 + x * 32, 32)
    wfull[k, rows] = over_z(b2)
    sb = gather(wfull.at[k, rows], NX, at_x)
    arrived(sc)
    sc = gather(wfull.at[k, rows_of(1024, z * 64, 64)], NZ, at_z)
    arrived(sa)
    sa = gather(wfull.at[k, rows_of(0, x * 128, 128)], NX, at_x)
    arrived(sb)
    sb = gather(wfull.at[k, rows_of(512, y * 128, 128)], NY, at_y)
    finals = []

    def hand_over(base, size, extent, me, copies):
        def give(owner):
            block = wfull.at[k, rows_of(base, owner * size, size)]
            finals.append(push(block, block, partner))

        give(me)
        order = sorted(range(1, extent), key=lambda d: min(d, extent - d))
        for d in order:
            copies[d - 1].wait_recv()
            give(lax.rem(me - d + extent, extent))

    hand_over(0, 128, NX, x, sa)
    hand_over(512, 128, NY, y, sb)
    hand_over(1024, 64, NZ, z, sc)
    arrived(finals)
    finish_gradient(i_high, i_low, t_high, t_low, cmat, wfull, m_high, m_low, xmat, top_v, out_top, local_sem, written)
    for copy in written:
        copy.wait()
    for copy in pending:
        copy.wait_send()


def odd(value, size):
    return value.reshape(HALF // (2 * size), 2, size, HALF)[:, 1].reshape(HALF // 2, HALF)


def inverse_pair(low, inv, which):
    rows, lanes = iota((HALF, HALF), 0), iota((HALF, HALF), 1)
    group = rows - lax.rem(rows, 8)
    within = iota((16, 8, HALF), 1)
    spans = [slice(which * BLOCK + HALF * i, which * BLOCK + HALF * i + HALF) for i in range(2)]
    owns = [low[span, span] for span in spans]
    values = [jnp.where(rows == lanes, 1.0, 0.0).reshape(16, 8, HALF)] * 2
    for step in range(8):
        for i in range(2):
            value = values[i]
            column = jnp.sum(jnp.where(lanes == group + step, owns[i], 0.0), axis=1, keepdims=True)
            column = jnp.broadcast_to(column, (HALF, HALF)).reshape(16, 8, HALF)
            solved = value[:, step : step + 1] / column[:, step : step + 1]
            solved = jnp.broadcast_to(solved, (16, 8, HALF))
            values[i] = jnp.where(within == step, solved, jnp.where(within > step, value - column * solved, value))
    values = [value.reshape(HALF, HALF) for value in values]
    for size in (8, 16, 32, 64):
        upper, left = lax.div(rows, size), lax.div(lanes, size)
        mask = jnp.logical_and(left + 1 == upper, lax.rem(upper, 2) == 1)
        inner = [dot6(odd(jnp.where(mask, owns[i], 0.0), size), values[i]) for i in range(2)]
        shape = (HALF // (2 * size), 1, size, HALF)
        none = jnp.zeros(shape, F32)
        inner = [jnp.concatenate([none, value.reshape(shape)], axis=1).reshape(HALF, HALF) for value in inner]
        inner = [dot6(odd(values[i], size), inner[i]) for i in range(2)]
        inner = [jnp.concatenate([none, value.reshape(shape)], axis=1).reshape(HALF, HALF) for value in inner]
        values = [values[i] - inner[i] for i in range(2)]
    first, second = spans
    inv[first, first] = values[0]
    inv[second, second] = values[1]
    inv[second, first] = -dot6(values[1], dot6(low[second, first], values[0]))
    inv[first, second] = jnp.zeros((HALF, HALF), F32)


def inverse_blocks(low, inv):
    one, two, three = slice(0, BLOCK), slice(BLOCK, 2 * BLOCK), slice(2 * BLOCK, 3 * BLOCK)
    inv[two, one] = -dot6(inv[two, two], dot6(low[two, one], inv[one, one]))
    inv[three, two] = -dot6(inv[three, three], dot6(low[three, two], inv[two, two]))
    inv[three, one] = -dot6(
        inv[three, three], dot6(low[three, one], inv[one, one]) + dot6(low[three, two], inv[two, one])
    )
    inv[one, 256:768] = jnp.zeros((BLOCK, 512), F32)
    inv[two, 512:768] = jnp.zeros((BLOCK, BLOCK), F32)


def inverse_halves(inv, i_high, i_low, t_high, t_low):
    for i in range(3):
        for j in range(i, 3):
            rows, lanes = slice(BLOCK * i, BLOCK * i + BLOCK), slice(BLOCK * j, BLOCK * j + BLOCK)
            value = inv[lanes, rows]
            i_high[lanes, rows], i_low[lanes, rows] = split(value)
            t_high[rows, lanes], t_low[rows, lanes] = split(value.T)


def start_gradient(low, topv, cmat):
    rows, lanes = iota((BLOCK, BLOCK), 0), iota((BLOCK, BLOCK), 1)
    for i in range(3):
        block = slice(BLOCK * i, BLOCK * i + BLOCK)
        flipped = low[BLOCK * i :, block].T
        for j in range(3):
            other = slice(BLOCK * j, BLOCK * j + BLOCK)
            if j > i:
                cmat[block, other] = jnp.zeros((BLOCK, BLOCK), F32)
                continue
            value = dot3(flipped, topv[BLOCK * i :, other])
            if i == j:
                value = jnp.where(rows > lanes, value, jnp.where(rows == lanes, 0.5 * value, 0.0))
            cmat[block, other] = value


def finish_gradient(i_high, i_low, t_high, t_low, cmat, wfull, m_high, m_low, xmat, top_v, out_top, local_sem, written):
    rows, lanes = iota((BLOCK, HALF), 0), iota((BLOCK, HALF), 1)
    for block in range(3):
        for side in range(2):
            start = OFFSETS[block]
            column = slice(BLOCK * block + HALF * side, BLOCK * block + HALF * side + HALF)
            value = wfull[side, start : start + BLOCK]
            place = lanes + HALF * side
            value = jnp.where(rows > place, value, jnp.where(rows == place, 0.5 * value, 0.0))
            cmat[BLOCK * block : BLOCK * block + BLOCK, column] -= value
            if block < 2:
                end = start + WIDTH - BLOCK * block
                cmat[BLOCK * block + BLOCK :, column] -= wfull[side, start + BLOCK : end]
    def three(left_high, left_low, right_high, right_low):
        dims = ((1,), (0,))
        return (
            contract(left_low, right_high, dims) + contract(left_high, right_low, dims) + contract(left_high, right_high, dims)
        )

    for j in range(3):
        other = slice(BLOCK * j, BLOCK * j + BLOCK)
        c_high, c_low = split(cmat[BLOCK * j :, other])
        for i in range(3):
            block, start = slice(BLOCK * i, BLOCK * i + BLOCK), BLOCK * max(i, j)
            skip = start - BLOCK * j
            value = three(t_high[block, start:], t_low[block, start:], c_high[skip:], c_low[skip:])
            m_high[block, other], m_low[block, other] = split(value)
    for j in range(3):
        block, start = slice(BLOCK * j, BLOCK * j + BLOCK), BLOCK * j
        xmat[:, block] = three(m_high[:, start:], m_low[:, start:], i_high[start:, block], i_low[start:, block])
    rows, lanes = iota((BLOCK, BLOCK), 0), iota((BLOCK, BLOCK), 1)
    for i in range(3):
        for j in range(3):
            block, other = slice(BLOCK * i, BLOCK * i + BLOCK), slice(BLOCK * j, BLOCK * j + BLOCK)
            if j > i:
                top_v[block, other] = jnp.zeros((BLOCK, BLOCK), F32)
                continue
            value = xmat[block, other] + xmat[other, block].T
            if i == j:
                value = jnp.where(rows > lanes, value, jnp.where(rows == lanes, 0.5 * value, 0.0))
            top_v[block, other] = value
        copy = pltpu.make_async_copy(top_v.at[block], out_top.at[block], local_sem.at[8 + i])
        copy.start()
        written.append(copy)


def deliver(rows_in, top_in, rows_out, top_out, rows_v, top_v, in_sem, out_sem):
    parts = [(rows_in, rows_v, rows_out)]
    for i in range(6):
        span = pl.ds(HALF * i, HALF)
        parts.append((top_in.at[span], top_v.at[span], top_out.at[span]))
    incoming = [pltpu.make_async_copy(part[0], part[1], in_sem.at[i]) for i, part in enumerate(parts)]
    outgoing = [pltpu.make_async_copy(part[1], part[2], out_sem.at[i]) for i, part in enumerate(parts)]
    for copy in incoming:
        copy.start()
    for before, after in zip(incoming, outgoing):
        before.wait()
        after.start()
    for copy in outgoing:
        copy.wait()


def per_device(trail_grad, factor_rows, factor_top, rows_grad, top_grad):
    anywhere = pl.BlockSpec(memory_space=pl.ANY)
    square, half_square = pltpu.VMEM((WIDTH, WIDTH), F32), pltpu.VMEM((WIDTH, WIDTH), BF16)

    def vmem(*shape):
        return pltpu.VMEM(shape, F32)

    shapes = (jax.ShapeDtypeStruct((64, WIDTH), F32), jax.ShapeDtypeStruct((WIDTH, WIDTH), F32))
    results = pl.pallas_call(
        kernel,
        out_shape=shapes,
        in_specs=[anywhere] * 5,
        out_specs=(anywhere, anywhere),
        scratch_shapes=[
            vmem(1024, 1024), pltpu.VMEM((1024, 1024), BF16), pltpu.VMEM((1024, 1024), BF16),
            vmem(WIDTH, 1024), vmem(4, GROUP, 1024), vmem(4, SUB, 1024), vmem(4, 8, SUB, 128), vmem(4, 4, SUB, 128),
            vmem(4, 4, SUB, 128), square, square, square, *[half_square] * 4, square, half_square, half_square, square, vmem(128, WIDTH), vmem(WIDTH, 128),
            vmem(128, WIDTH), vmem(NZ, CHUNK, 128), vmem(WIDTH, 128), vmem(1536, 128), vmem(3, 128, 128), vmem(3, 32, 128), vmem(128, 128),
            vmem(8, 32, 128), vmem(3, 128, 128), vmem(3, 32, 128), vmem(128, 128), vmem(8, 32, 128), vmem(7, 64, 128),
            vmem(3, 16, 128), vmem(64, 128), vmem(4, 16, 128), vmem(2, 1536, 128), vmem(64, WIDTH), square, pltpu.SemaphoreType.DMA((11,)),
            pltpu.SemaphoreType.DMA((SEMAPHORES,)), pltpu.SemaphoreType.DMA((SEMAPHORES,)),
        ],
        compiler_params=pltpu.CompilerParams(collective_id=0, has_side_effects=True, vmem_limit_bytes=62 << 20),
    )(trail_grad, factor_rows.T, factor_top, rows_grad, top_grad)
    return pl.pallas_call(
        deliver,
        out_shape=shapes,
        in_specs=[anywhere] * 2,
        out_specs=(anywhere, anywhere),
        scratch_shapes=[vmem(64, WIDTH), square, pltpu.SemaphoreType.DMA((7,)), pltpu.SemaphoreType.DMA((7,))],
    )(*results)


def solution(mesh):
    placed = (P("row", "col"), P("col", "row"), P(), P(("row", "col"), None), P())
    return jax.shard_map(
        per_device,
        mesh=mesh,
        in_specs=placed,
        out_specs=(P(("row", "col"), None), P()),
        check_vma=False,
    )
```

```python
import jax
import jax.numpy as jnp
from jax import lax
from jax.experimental import pallas as pl
from jax.experimental.pallas import tpu as pltpu
from jax.sharding import PartitionSpec as P

MESH = pl.DeviceIdType.MESH
F32, BF16 = jnp.float32, jnp.bfloat16
HIGHEST = lax.Precision.HIGHEST
NX, NY, NZ = 4, 4, 8
BLOCK, HALF, WIDTH = 256, 128, 768
CHUNK, PIECE = 48, 24
GROUP, SUB = 192, 96
OFFSETS = (0, 768, 1280)
SEMAPHORES = 200


def contract(left, right, dims, precision=None):
    return lax.dot_general(left, right, (dims, ((), ())), precision=precision, preferred_element_type=F32)


def split(value):
    high = value.astype(BF16)
    return high, (value - high.astype(F32)).astype(BF16)


def dot3(left, right, dims=((1,), (0,))):
    left_high, left_low = split(left)
    right_high, right_low = split(right)
    return (
        contract(left_low, right_high, dims)
        + contract(left_high, right_low, dims)
        + contract(left_high, right_high, dims)
    )


def dot6(left, right):
    return contract(left, right, ((1,), (0,)), HIGHEST)


def iota(shape, dim):
    return lax.broadcasted_iota(jnp.int32, shape, dim)


def aligned(index, unit):
    return pl.multiple_of(index * unit, unit)


def kernel(trail, factor, lower, grad, top, out_rows, out_top, strail, s_high, s_low, f_all, zt, cx, zc, r_left, r_right, low, topv,
           inv, i_high, i_low, t_high, t_low, cmat, m_high, m_low, xmat, gbuf, p_hat, p_rows, planes, f_here, wst, r_a1, r_a2, a1, a2, r_b1, r_b2, b1, b2, r_c1, r_c2, c1, c2,
           wfull, rows_v, top_v, local_sem, send_sem, recv_sem):
    row, col = lax.axis_index("row"), lax.axis_index("col")
    y, x = lax.div(row, NX), lax.rem(row, NX)
    z, k = lax.div(col, 2), lax.rem(col, 2)
    other = 1 - k

    def at_x(d):
        return (y * NX + lax.rem(x + d + NX, NX), col)

    def at_y(d):
        return (lax.rem(y + d + NY, NY) * NX + x, col)

    def at_z(d):
        return (row, lax.rem(z + d + NZ, NZ) * 2 + k)

    partner = (row, z * 2 + other)
    count = [0]
    pending = []

    def push(src, dst, device):
        slot = count[0]
        count[0] += 1
        copy = pltpu.make_async_remote_copy(
            src_ref=src, dst_ref=dst, send_sem=send_sem.at[slot], recv_sem=recv_sem.at[slot], device_id=device, device_id_type=MESH
        )
        copy.start()
        pending.append(copy)
        return copy

    local = [
        pltpu.make_async_copy(factor, f_all.at[pl.ds(aligned(row, CHUNK), CHUNK)], local_sem.at[0]),
        pltpu.make_async_copy(grad, gbuf.at[pl.ds(aligned(k, 64), 64)], local_sem.at[1]),
        pltpu.make_async_copy(trail, strail, local_sem.at[2]),
        pltpu.make_async_copy(lower, low, local_sem.at[3]),
        pltpu.make_async_copy(top, topv, local_sem.at[4]),
    ]
    for copy in local:
        copy.start()

    barrier = pltpu.get_barrier_semaphore()

    def greet(device):
        pl.semaphore_signal(barrier, inc=1, device_id=device, device_id_type=MESH)

    for d in range(1, NX * NY):
        greet((lax.rem(row + d, NX * NY), col))
    for d in range(1, NZ):
        greet(at_z(d))
    greet(partner)
    pl.semaphore_wait(barrier, NX * NY + NZ - 1)

    local[0].wait()
    local[1].wait()

    rings = {"x": at_x, "y": at_y}

    def piece(ring, item, shift):
        if ring == "x":
            owner_x, owner_y = lax.rem(x + shift + NX, NX), y if item == 0 else lax.rem(y + item - 1, NY)
            offset = 0 if item == 0 else PIECE
        else:
            owner_y, owner_x = lax.rem(y + shift + NY, NY), x if item == 0 else lax.rem(x + item - 1, NX)
            offset = PIECE if item == 0 else 0
        return pl.ds(pl.multiple_of((owner_y * NX + owner_x) * CHUNK + offset, 8), PIECE)

    full, halves = {}, {}

    def send(ring, item):
        rows = f_all.at[piece(ring, item, 0)]
        full[ring, item] = [push(rows, rows, rings[ring](1)), push(rows, rows, rings[ring](-1))]

    def forward(ring, item):
        from_left, from_right = full[ring, item]
        from_left.wait_recv()
        rows = f_all.at[piece(ring, item, -1), pl.ds(0, 512)]
        right = push(rows, rows, rings[ring](1))
        from_right.wait_recv()
        rows = f_all.at[piece(ring, item, 1), pl.ds(512, 512)]
        halves[ring, item] = [right, push(rows, rows, rings[ring](-1))]

    def settle(ring, item):
        for copy in halves[ring, item]:
            copy.wait_recv()

    send("x", 0), send("y", 0), send("x", 1), send("y", 1)
    own_half = pl.ds(aligned(k, 64), 64)
    grad_copy = push(gbuf.at[own_half], gbuf.at[own_half], partner)
    chunk = pl.ds(aligned(row, CHUNK), CHUNK)
    spread = []
    for d in range(1, NZ):
        lanes = pl.ds(aligned(lax.rem(z + d, NZ), 128), 128)
        spread.append(push(f_all.at[chunk, lanes], planes.at[z], at_z(d)))
    keep = pltpu.make_async_copy(f_all.at[chunk, pl.ds(aligned(z, 128), 128)], planes.at[z], local_sem.at[5])
    keep.start()
    owner = lax.rem(row, 2) == k
    landing = f_here.at[chunk]
    pair = lax.div(row, 2)
    exchange, first_move, first_stay = [], [], []

    def rearrange():
        keep.wait()
        for copy in spread:
            copy.wait_recv()
        for d in range(NZ):
            block = lax.rem(pair + d, NZ)
            copy = pltpu.make_async_remote_copy(
                src_ref=planes.at[block], dst_ref=landing, send_sem=send_sem.at[SEMAPHORES - 2 - d],
                recv_sem=recv_sem.at[SEMAPHORES - 1], device_id=(block * 2 + k, col), device_id_type=MESH,
            )
            if d == 0:
                first_move.append(copy)
                first_stay.append(pltpu.make_async_copy(planes.at[block], landing, local_sem.at[6]))
            else:
                copy.start()
                exchange.append(copy)

        @pl.when(jnp.logical_not(owner))
        def _():
            first_move[0].start()

        @pl.when(owner)
        def _():
            first_stay[0].start()

    share = pltpu.make_async_remote_copy(
        src_ref=f_here, dst_ref=f_here, send_sem=send_sem.at[SEMAPHORES - 10], recv_sem=recv_sem.at[SEMAPHORES - 10],
        device_id=partner, device_id_type=MESH,
    )

    def pass_on():
        for copy in exchange:
            copy.wait_send()

        @pl.when(owner)
        def _():
            most = f_here.at[0 : WIDTH - CHUNK]
            pltpu.make_async_remote_copy(
                src_ref=most, dst_ref=most, send_sem=send_sem.at[SEMAPHORES - 1], recv_sem=recv_sem.at[SEMAPHORES - 1],
                device_id=partner, device_id_type=MESH,
            ).wait_recv()
            first_stay[0].wait()
            share.start()

        @pl.when(jnp.logical_not(owner))
        def _():
            first_move[0].wait_send()

    def passed():
        @pl.when(owner)
        def _():
            share.wait_send()

        @pl.when(jnp.logical_not(owner))
        def _():
            share.wait_recv()

    local[2].wait()

    @pl.loop(0, 8)
    def _(step):
        rows = pl.ds(aligned(step, 128), 128)
        s_high[rows], s_low[rows] = split(strail[rows])

    forward("x", 0), forward("y", 0)
    send("x", 2), send("y", 2)
    forward("x", 1), forward("y", 1)
    send("x", 4), send("y", 4)
    settle("x", 0), settle("y", 0)
    send("x", 3), send("y", 3)
    grad_copy.wait_recv()
    cmat[:, 0:128] = gbuf[...].T
    for j in range(4):
        rows = pl.ds(pl.multiple_of(j * GROUP + k * SUB, 8), SUB)
        p_hat[rows] = cmat[rows, 0:128]
    settle("x", 1)

    def multiply(*groups):
        parts = [split(f_all[pl.ds(aligned(lax.rem(y + j, NY), GROUP), GROUP)]) for j in groups]
        high = jnp.concatenate([part[0] for part in parts], axis=0)
        both = jnp.concatenate([part[0] for part in parts] + [part[1] for part in parts], axis=0)
        size = GROUP * len(groups)

        @pl.loop(0, 4)
        def _(step):
            part = pl.ds(aligned(step, BLOCK), BLOCK)
            dims = ((1,), (1,))
            first = contract(both, s_high[part], dims)
            value = first[:size] + first[size:] + contract(high, s_low[part], dims)
            for i, j in enumerate(groups):
                zt[j, :, part] = value[GROUP * i : GROUP * i + GROUP]

    crossing = {}

    def cross(j):
        crossing[j] = push(zt.at[j, pl.ds(aligned(other, SUB), SUB)], cx.at[j], partner)

    lefts, rights = {}, {}

    def begin(j):
        crossing[j].wait_recv()
        own = pl.ds(aligned(k, SUB), SUB)
        for d in range(NZ):
            lanes = pl.ds(128 * d, 128)
            zc[j, d] = zt[j, own, lanes] + cx[j, :, lanes]
        far = lax.rem(z + 4, NZ)
        lefts[j] = push(zc.at[j, far, pl.ds(0, 48)], r_left.at[j, 0, pl.ds(0, 48)], at_z(-1))
        rights[j] = push(zc.at[j, far, pl.ds(48, 48)], r_right.at[j, 0, pl.ds(48, 48)], at_z(1))

    def travel(j, step):
        to_left, to_right = lax.rem(z + 3 + step, NZ), lax.rem(z + 5 - step, NZ)
        lefts[j].wait_recv()
        if step == 2:
            zc[j, to_left, 0:48] += r_left[j, 0, 0:48]
        else:
            zc[j, to_left] += r_left[j, step - 2]
        lefts[j] = push(zc.at[j, to_left], r_left.at[j, step - 1], at_z(-1))
        rights[j].wait_recv()
        if step == 2:
            zc[j, to_right, 48:96] += r_right[j, 0, 48:96]
        else:
            zc[j, to_right] += r_right[j, step - 2]
        rights[j] = push(zc.at[j, to_right], r_right.at[j, step - 1], at_z(1))

    shares = []

    def arrive(j):
        lefts[j].wait_recv()
        rights[j].wait_recv()
        rows = pl.ds(pl.multiple_of(lax.rem(y + j, NY) * GROUP + k * SUB, 8), SUB)
        p_hat[rows] = p_hat[rows] - 2.0 * (zc[j, z] + r_left[j, 3] + r_right[j, 3])
        shares.append(push(p_hat.at[rows], p_hat.at[rows], partner))

    multiply(0)
    cross(0)
    forward("x", 2), forward("y", 2), forward("x", 4), forward("y", 4)
    begin(0)
    forward("x", 3), forward("y", 3)
    rearrange()
    travel(0, 2)
    settle("x", 2), settle("x", 4)
    multiply(1, 3)
    cross(1)
    cross(3)
    travel(0, 3)
    for ring, item in (("y", 1), ("y", 2), ("y", 3), ("y", 4), ("x", 3)):
        settle(ring, item)
    begin(1)
    begin(3)
    multiply(2)
    cross(2)
    travel(0, 4)
    pass_on()
    begin(2)
    travel(1, 2)
    travel(3, 2)
    arrive(0)
    travel(2, 2)
    local[3].wait()
    inverse_pair(low, inv, 0)
    travel(1, 3)
    travel(3, 3)
    travel(2, 3)
    travel(1, 4)
    travel(3, 4)
    travel(2, 4)
    arrive(1)
    arrive(3)
    arrive(2)
    for copy in shares:
        copy.wait_recv()
    passed()

    for block in range(3):
        start = OFFSETS[block]
        rows = WIDTH - BLOCK * block
        wst[start : start + rows] = dot3(p_hat[BLOCK * block :], f_here[pl.ds(pl.multiple_of(block * BLOCK + k * HALF, HALF), HALF)], ((1,), (1,)))

    def scatter(src, unit, extent, reach, me, buffer):
        copies = []
        for d in range(1, extent):
            to = lax.rem(me + d, extent)
            copies.append(push(src(to), buffer.at[d - 1], reach(d)))
        return copies

    def total(own, copies, buffer):
        for d, copy in enumerate(copies):
            copy.wait_recv()
            own = own + buffer[d]
        return own

    def gather(ref, extent, reach):
        return [push(ref, ref, reach(d)) for d in range(1, extent)]

    def arrived(copies):
        for copy in copies:
            copy.wait_recv()

    def rows_of(base, start, size):
        return pl.ds(pl.multiple_of(base + start, 8), size)

    sc = scatter(lambda to: wst.at[rows_of(1024, to * 64, 64)], 64, NZ, at_z, z, r_c1)
    sa = scatter(lambda to: wst.at[rows_of(0, to * 128, 128)], 128, NX, at_x, x, r_a1)
    sb = scatter(lambda to: wst.at[rows_of(512, to * 128, 128)], 128, NY, at_y, y, r_b1)
    p_rows[...] = p_hat[...].T
    inverse_pair(low, inv, 1)
    a1[...] = total(wst[rows_of(0, x * 128, 128)], sa, r_a1)
    sa = scatter(lambda to: a1.at[rows_of(0, to * 32, 32)], 32, NY, at_y, y, r_a2)
    b1[...] = total(wst[rows_of(512, y * 128, 128)], sb, r_b1)
    sb = scatter(lambda to: b1.at[rows_of(0, to * 32, 32)], 32, NX, at_x, x, r_b2)
    inverse_pair(low, inv, 2)
    a2[z] = total(a1[rows_of(0, y * 32, 32)], sa, r_a2)
    sa = gather(a2.at[z], NZ, at_z)
    b2[z] = total(b1[rows_of(0, x * 32, 32)], sb, r_b2)
    sb = gather(b2.at[z], NZ, at_z)
    c1[...] = total(wst[rows_of(1024, z * 64, 64)], sc, r_c1)
    sc = scatter(lambda to: c1.at[rows_of(0, to * 16, 16)], 16, NX, at_x, x, r_c2)
    inverse_blocks(low, inv)
    c2[y] = total(c1[rows_of(0, x * 16, 16)], sc, r_c2)
    sc = gather(c2.at[y], NY, at_y)
    inverse_halves(inv, i_high, i_low, t_high, t_low)
    local[4].wait()
    start_gradient(low, topv, cmat)
    arrived(sc)
    rows = rows_of(1024, z * 64 + x * 16, 16)
    wfull[k, rows] = c2[0] + c2[1] + c2[2] + c2[3]
    sc = gather(wfull.at[k, rows], NX, at_x)
    rows_v[...] = dot6(p_rows[pl.ds(aligned(k, 64), 64)], inv[...])
    written = [pltpu.make_async_copy(rows_v, out_rows, local_sem.at[7])]
    written[0].start()

    def over_z(ref):
        value = ref[0]
        for d in range(1, NZ):
            value = value + ref[d]
        return value

    arrived(sa)
    rows = rows_of(0, x * 128 + y * 32, 32)
    wfull[k, rows] = over_z(a2)
    sa = gather(wfull.at[k, rows], NY, at_y)
    arrived(sb)
    rows = rows_of(512, y * 128 + x * 32, 32)
    wfull[k, rows] = over_z(b2)
    sb = gather(wfull.at[k, rows], NX, at_x)
    arrived(sc)
    sc = gather(wfull.at[k, rows_of(1024, z * 64, 64)], NZ, at_z)
    arrived(sa)
    sa = gather(wfull.at[k, rows_of(0, x * 128, 128)], NX, at_x)
    arrived(sb)
    sb = gather(wfull.at[k, rows_of(512, y * 128, 128)], NY, at_y)
    finals = []

    def hand_over(base, size, extent, me, copies):
        def give(owner):
            block = wfull.at[k, rows_of(base, owner * size, size)]
            finals.append(push(block, block, partner))

        give(me)
        order = sorted(range(1, extent), key=lambda d: min(d, extent - d))
        for d in order:
            copies[d - 1].wait_recv()
            give(lax.rem(me - d + extent, extent))

    hand_over(0, 128, NX, x, sa)
    hand_over(512, 128, NY, y, sb)
    hand_over(1024, 64, NZ, z, sc)
    arrived(finals)
    finish_gradient(i_high, i_low, t_high, t_low, cmat, wfull, m_high, m_low, xmat, top_v, out_top, local_sem, written)
    for copy in written:
        copy.wait()
    for copy in pending:
        copy.wait_send()


def odd(value, size):
    return value.reshape(HALF // (2 * size), 2, size, HALF)[:, 1].reshape(HALF // 2, HALF)


def inverse_pair(low, inv, which):
    rows, lanes = iota((HALF, HALF), 0), iota((HALF, HALF), 1)
    group = rows - lax.rem(rows, 8)
    within = iota((16, 8, HALF), 1)
    spans = [slice(which * BLOCK + HALF * i, which * BLOCK + HALF * i + HALF) for i in range(2)]
    owns = [low[span, span] for span in spans]
    values = [jnp.where(rows == lanes, 1.0, 0.0).reshape(16, 8, HALF)] * 2
    for step in range(8):
        for i in range(2):
            value = values[i]
            column = jnp.sum(jnp.where(lanes == group + step, owns[i], 0.0), axis=1, keepdims=True)
            column = jnp.broadcast_to(column, (HALF, HALF)).reshape(16, 8, HALF)
            solved = value[:, step : step + 1] / column[:, step : step + 1]
            solved = jnp.broadcast_to(solved, (16, 8, HALF))
            values[i] = jnp.where(within == step, solved, jnp.where(within > step, value - column * solved, value))
    values = [value.reshape(HALF, HALF) for value in values]
    for size in (8, 16, 32, 64):
        upper, left = lax.div(rows, size), lax.div(lanes, size)
        mask = jnp.logical_and(left + 1 == upper, lax.rem(upper, 2) == 1)
        inner = [dot6(odd(jnp.where(mask, owns[i], 0.0), size), values[i]) for i in range(2)]
        shape = (HALF // (2 * size), 1, size, HALF)
        none = jnp.zeros(shape, F32)
        inner = [jnp.concatenate([none, value.reshape(shape)], axis=1).reshape(HALF, HALF) for value in inner]
        inner = [dot6(odd(values[i], size), inner[i]) for i in range(2)]
        inner = [jnp.concatenate([none, value.reshape(shape)], axis=1).reshape(HALF, HALF) for value in inner]
        values = [values[i] - inner[i] for i in range(2)]
    first, second = spans
    inv[first, first] = values[0]
    inv[second, second] = values[1]
    inv[second, first] = -dot6(values[1], dot6(low[second, first], values[0]))
    inv[first, second] = jnp.zeros((HALF, HALF), F32)


def inverse_blocks(low, inv):
    one, two, three = slice(0, BLOCK), slice(BLOCK, 2 * BLOCK), slice(2 * BLOCK, 3 * BLOCK)
    inv[two, one] = -dot6(inv[two, two], dot6(low[two, one], inv[one, one]))
    inv[three, two] = -dot6(inv[three, three], dot6(low[three, two], inv[two, two]))
    inv[three, one] = -dot6(
        inv[three, three], dot6(low[three, one], inv[one, one]) + dot6(low[three, two], inv[two, one])
    )
    inv[one, 256:768] = jnp.zeros((BLOCK, 512), F32)
    inv[two, 512:768] = jnp.zeros((BLOCK, BLOCK), F32)


def inverse_halves(inv, i_high, i_low, t_high, t_low):
    for i in range(3):
        for j in range(i, 3):
            rows, lanes = slice(BLOCK * i, BLOCK * i + BLOCK), slice(BLOCK * j, BLOCK * j + BLOCK)
            value = inv[lanes, rows]
            i_high[lanes, rows], i_low[lanes, rows] = split(value)
            t_high[rows, lanes], t_low[rows, lanes] = split(value.T)


def start_gradient(low, topv, cmat):
    rows, lanes = iota((BLOCK, BLOCK), 0), iota((BLOCK, BLOCK), 1)
    for i in range(3):
        block = slice(BLOCK * i, BLOCK * i + BLOCK)
        flipped = low[BLOCK * i :, block].T
        for j in range(3):
            other = slice(BLOCK * j, BLOCK * j + BLOCK)
            if j > i:
                cmat[block, other] = jnp.zeros((BLOCK, BLOCK), F32)
                continue
            value = dot3(flipped, topv[BLOCK * i :, other])
            if i == j:
                value = jnp.where(rows > lanes, value, jnp.where(rows == lanes, 0.5 * value, 0.0))
            cmat[block, other] = value


def finish_gradient(i_high, i_low, t_high, t_low, cmat, wfull, m_high, m_low, xmat, top_v, out_top, local_sem, written):
    rows, lanes = iota((BLOCK, HALF), 0), iota((BLOCK, HALF), 1)
    for block in range(3):
        for side in range(2):
            start = OFFSETS[block]
            column = slice(BLOCK * block + HALF * side, BLOCK * block + HALF * side + HALF)
            value = wfull[side, start : start + BLOCK]
            place = lanes + HALF * side
            value = jnp.where(rows > place, value, jnp.where(rows == place, 0.5 * value, 0.0))
            cmat[BLOCK * block : BLOCK * block + BLOCK, column] -= value
            if block < 2:
                end = start + WIDTH - BLOCK * block
                cmat[BLOCK * block + BLOCK :, column] -= wfull[side, start + BLOCK : end]
    def three(left_high, left_low, right_high, right_low):
        dims = ((1,), (0,))
        return (
            contract(left_low, right_high, dims) + contract(left_high, right_low, dims) + contract(left_high, right_high, dims)
        )

    for j in range(3):
        other = slice(BLOCK * j, BLOCK * j + BLOCK)
        c_high, c_low = split(cmat[BLOCK * j :, other])
        for i in range(3):
            block, start = slice(BLOCK * i, BLOCK * i + BLOCK), BLOCK * max(i, j)
            skip = start - BLOCK * j
            value = three(t_high[block, start:], t_low[block, start:], c_high[skip:], c_low[skip:])
            m_high[block, other], m_low[block, other] = split(value)
    for j in range(3):
        block, start = slice(BLOCK * j, BLOCK * j + BLOCK), BLOCK * j
        xmat[:, block] = three(m_high[:, start:], m_low[:, start:], i_high[start:, block], i_low[start:, block])
    rows, lanes = iota((BLOCK, BLOCK), 0), iota((BLOCK, BLOCK), 1)
    for i in range(3):
        for j in range(3):
            block, other = slice(BLOCK * i, BLOCK * i + BLOCK), slice(BLOCK * j, BLOCK * j + BLOCK)
            if j > i:
                top_v[block, other] = jnp.zeros((BLOCK, BLOCK), F32)
                continue
            value = xmat[block, other] + xmat[other, block].T
            if i == j:
                value = jnp.where(rows > lanes, value, jnp.where(rows == lanes, 0.5 * value, 0.0))
            top_v[block, other] = value
        copy = pltpu.make_async_copy(top_v.at[block], out_top.at[block], local_sem.at[8 + i])
        copy.start()
        written.append(copy)


def deliver(rows_in, top_in, rows_out, top_out, rows_v, top_v, in_sem, out_sem):
    parts = [(rows_in, rows_v, rows_out)]
    for i in range(6):
        span = pl.ds(HALF * i, HALF)
        parts.append((top_in.at[span], top_v.at[span], top_out.at[span]))
    incoming = [pltpu.make_async_copy(part[0], part[1], in_sem.at[i]) for i, part in enumerate(parts)]
    outgoing = [pltpu.make_async_copy(part[1], part[2], out_sem.at[i]) for i, part in enumerate(parts)]
    for copy in incoming:
        copy.start()
    for before, after in zip(incoming, outgoing):
        before.wait()
        after.start()
    for copy in outgoing:
        copy.wait()


def per_device(trail_grad, factor_rows, factor_top, rows_grad, top_grad):
    anywhere = pl.BlockSpec(memory_space=pl.ANY)
    square, half_square = pltpu.VMEM((WIDTH, WIDTH), F32), pltpu.VMEM((WIDTH, WIDTH), BF16)

    def vmem(*shape):
        return pltpu.VMEM(shape, F32)

    shapes = (jax.ShapeDtypeStruct((64, WIDTH), F32), jax.ShapeDtypeStruct((WIDTH, WIDTH), F32))
    results = pl.pallas_call(
        kernel,
        out_shape=shapes,
        in_specs=[anywhere] * 5,
        out_specs=(anywhere, anywhere),
        scratch_shapes=[
            vmem(1024, 1024), pltpu.VMEM((1024, 1024), BF16), pltpu.VMEM((1024, 1024), BF16),
            vmem(WIDTH, 1024), vmem(4, GROUP, 1024), vmem(4, SUB, 1024), vmem(4, 8, SUB, 128), vmem(4, 4, SUB, 128),
            vmem(4, 4, SUB, 128), square, square, square, *[half_square] * 4, square, half_square, half_square, square, vmem(128, WIDTH), vmem(WIDTH, 128),
            vmem(128, WIDTH), vmem(NZ, CHUNK, 128), vmem(WIDTH, 128), vmem(1536, 128), vmem(3, 128, 128), vmem(3, 32, 128), vmem(128, 128),
            vmem(8, 32, 128), vmem(3, 128, 128), vmem(3, 32, 128), vmem(128, 128), vmem(8, 32, 128), vmem(7, 64, 128),
            vmem(3, 16, 128), vmem(64, 128), vmem(4, 16, 128), vmem(2, 1536, 128), vmem(64, WIDTH), square, pltpu.SemaphoreType.DMA((11,)),
            pltpu.SemaphoreType.DMA((SEMAPHORES,)), pltpu.SemaphoreType.DMA((SEMAPHORES,)),
        ],
        compiler_params=pltpu.CompilerParams(collective_id=0, has_side_effects=True, vmem_limit_bytes=62 << 20),
    )(trail_grad, factor_rows.T, factor_top, rows_grad, top_grad)
    return pl.pallas_call(
        deliver,
        out_shape=shapes,
        in_specs=[anywhere] * 2,
        out_specs=(anywhere, anywhere),
        scratch_shapes=[vmem(64, WIDTH), square, pltpu.SemaphoreType.DMA((7,)), pltpu.SemaphoreType.DMA((7,))],
    )(*results)


def solution(mesh):
    placed = (P("row", "col"), P("col", "row"), P(), P(("row", "col"), None), P())
    return jax.shard_map(
        per_device,
        mesh=mesh,
        in_specs=placed,
        out_specs=(P(("row", "col"), None), P()),
        check_vma=False,
    )
```
